32 devices in a mesh: groups: 2 (over y), row: 4 (over z), col: 4 (over x, core).
Axes of the slice: x: 2, y: 2, z: 4, core: 2. Of those that a mesh axis runs over, the one named last changes fastest.
Arguments:
- right_side: float32 [128, 8192], P('groups', ('row', 'col')), parts along dimension 0, may hold values from -6 to 6
- prior: float32 [8192], P(('row', 'col')), may hold values from 0.5 to 2
- blocks: bfloat16 [1024, 128, 128], P(('row', 'col')), may hold values from -0.125 to 0.125
- block_row: int32 [1024], P(('row', 'col')), may hold values from 0 to 63, as said below
- block_col: int32 [1024], P(('row', 'col')), may hold values from 0 to 63, as said below
Outputs:
- solution_field: float32 [128, 8192], P('groups', ('row', 'col')), parts along dimension 0
- residual: float32 [128, 8192], P('groups', ('row', 'col')), parts along dimension 0
The draws below stay inside these ranges and needn't reach their ends.
There are 2 independent parts, one for each index of `groups`. The reference program is written for one: setup_inputs(seed, part) draws one part's arguments, and reference() takes and returns one part's arrays. A program takes and returns all parts, laid end to end along the dimension named above; an argument that names none is the same for every part. Nothing has to cross between parts.
Inputs may be any that keep to these rules, and one draw needn't show every extreme that they name: `block_row`: stored blocks k*64 to (k+1)*64 - 1 belong to device k of row+col, k = r*4+c; their block rows lie in r*16 to (r+1)*16 - 1. `block_col`: the block columns b of device (r, c) satisfy (b // 4) % 4 == c.
All inputs are finite; a program needn't handle non-finite values.
Results may differ from the reference program's by a relative error of at most 0.0069.
Values may be sent and summed in bfloat16 or wider, within the bound.
A program may use at most 64 MiB of HBM per device.

```python
import math
import jax
import jax.numpy as jnp
from jax import lax

BLOCK = 128
FRAMES = 64
CB = 4
KB = 64
ITERS = 2
GRID_ROWS = 4
GRID_COLS = 4
ROWBLK = 16
NBLK = 64
NPIX = 8192
NNZ = 1024


def draw_block_row(key, part):
    device = jnp.arange(NNZ, dtype=jnp.int32) // KB
    position = jnp.arange(NNZ, dtype=jnp.int32) % KB
    grid_row = device // GRID_COLS
    offset_row = jax.random.randint(jax.random.fold_in(key, 11), (NNZ,), 0, ROWBLK, dtype=jnp.int32)
    offset_row = jnp.where(position == 0, 0, offset_row)
    offset_row = jnp.where(position == KB - 1, ROWBLK - 1, offset_row)
    return (grid_row * ROWBLK + offset_row).astype(jnp.int32)


def draw_block_col(key, part):
    key_stretch, key_inner = jax.random.split(jax.random.fold_in(key, 23))
    device = jnp.arange(NNZ, dtype=jnp.int32) // KB
    position = jnp.arange(NNZ, dtype=jnp.int32) % KB
    grid_col = device % GRID_COLS
    stretch_row = jax.random.randint(key_stretch, (NNZ,), 0, GRID_ROWS, dtype=jnp.int32)
    inner = jax.random.randint(key_inner, (NNZ,), 0, CB, dtype=jnp.int32)
    stretch_row = jnp.where(position == 0, 0, stretch_row)
    inner = jnp.where(position == 0, 0, inner)
    stretch_row = jnp.where(position == KB - 1, GRID_ROWS - 1, stretch_row)
    inner = jnp.where(position == KB - 1, CB - 1, inner)
    return ((stretch_row * GRID_COLS + grid_col) * CB + inner).astype(jnp.int32)


def block_scale(own_key, shape, cuts, low, high):
    factor_of = 1.0
    for axis_at, shards_of in cuts:
        heights = jax.random.uniform(jax.random.fold_in(jax.random.fold_in(own_key, 6), axis_at), (shards_of,), jnp.float32, low / len(cuts), high / len(cuts))
        factor_of = factor_of * jnp.repeat(jnp.exp(heights), shape[axis_at] // shards_of).reshape((-1,) + (1,) * (len(shape) - 1 - axis_at))
    return factor_of


def bell_draw(own_key, shape, scale, bound, pieces=(), kind=jnp.bfloat16):
    values = scale * jax.random.normal(own_key, shape, jnp.float32)
    if pieces:
        values = values * block_scale(own_key, shape, pieces, -0.22, 0.18)
    return jnp.clip(values, -bound, bound).astype(kind)


def setup_inputs(seed: int = 0, part: int = 0) -> dict:
    arg_keys = jax.random.split(jax.random.key(seed), 6)
    part_splits = jax.random.split(jax.random.fold_in(arg_keys[5], part), 6)
    return {
        "right_side": bell_draw(part_splits[0], (FRAMES, NPIX), 1.0, 6.0, ((1, 16),), jnp.float32),
        "prior": jnp.clip(jnp.exp(math.log(2.0) - 1.3862944 * jax.random.uniform(arg_keys[1], (NPIX,), jnp.float32) ** block_scale(arg_keys[1], (NPIX,), ((0, 16),), -0.2, 0.2)), 0.5, 2.0),
        "blocks": bell_draw(arg_keys[2], (NNZ, BLOCK, BLOCK), (KB // CB * BLOCK) ** -0.5, 0.125, ((0, 16),)),
        "block_row": draw_block_row(jax.random.fold_in(arg_keys[5], 71), part),
        "block_col": draw_block_col(jax.random.fold_in(arg_keys[5], 71), part),
    }


def spd_solve(matrix, rhs):
    factor = jnp.linalg.cholesky(matrix)
    half_solved = lax.linalg.triangular_solve(factor, rhs, left_side=True, lower=True)
    return lax.linalg.triangular_solve(factor, half_solved, left_side=True, lower=True, transpose_a=True)

def pair_gram(left, right):
    return lax.dot_general(left.astype(jnp.float32), right.astype(jnp.float32), (((1,), (1,)), ((), ())), precision=lax.Precision.HIGHEST, preferred_element_type=jnp.float32)

def apply_left(coeffs, panel):
    return jnp.dot(coeffs.astype(jnp.float32), panel.astype(jnp.float32), precision=lax.Precision.HIGHEST, preferred_element_type=jnp.float32)

def operator(grouped, prior, direction):
    search = direction.astype(jnp.bfloat16).astype(jnp.float32)
    panel_view = search.reshape(FRAMES, NBLK, BLOCK)

    def forward_step(total, stacked):
        tile_set, row_ids, col_ids = stacked
        picked = jnp.take(panel_view, col_ids, axis=1)
        contrib = jnp.einsum('fkj,kij->kfi', picked, tile_set.astype(jnp.float32), precision=lax.Precision.HIGHEST)
        return (total.at[row_ids].add(contrib), None)
    total, _ = lax.scan(forward_step, jnp.zeros((NBLK, FRAMES, BLOCK), jnp.float32), grouped)
    footprint = total.transpose(1, 0, 2).reshape(FRAMES, NPIX).astype(jnp.bfloat16).astype(jnp.float32)
    foot_view = footprint.reshape(FRAMES, NBLK, BLOCK)

    def backward_step(total, stacked):
        tile_set, row_ids, col_ids = stacked
        picked = jnp.take(foot_view, row_ids, axis=1)
        contrib = jnp.einsum('fki,kij->kfj', picked, tile_set.astype(jnp.float32), precision=lax.Precision.HIGHEST)
        return (total.at[col_ids].add(contrib), None)
    total, _ = lax.scan(backward_step, jnp.zeros((NBLK, FRAMES, BLOCK), jnp.float32), grouped)
    return total.transpose(1, 0, 2).reshape(FRAMES, NPIX) + prior[None, :] * direction

def reference(right_side, prior, blocks, block_row, block_col):
    devices = GRID_ROWS * GRID_COLS
    grouped = (blocks.reshape(devices, KB, BLOCK, BLOCK), block_row.reshape(devices, KB).astype(jnp.int32), block_col.reshape(devices, KB).astype(jnp.int32))
    solution = jnp.zeros_like(right_side)
    residual = right_side
    direction = right_side
    gram = pair_gram(residual, residual)
    for iteration in range(ITERS):
        image = operator(grouped, prior, direction)
        curvature = pair_gram(direction, image)
        step_alpha = spd_solve(curvature, gram)
        solution = solution + apply_left(step_alpha.T, direction)
        residual = residual - apply_left(step_alpha.T, image)
        if iteration + 1 < ITERS:
            new_gram = pair_gram(residual, residual)
            step_beta = spd_solve(gram, new_gram)
            direction = residual + apply_left(step_beta.T, direction)
            gram = new_gram
    return (solution, residual)
```

```python
import functools

import jax
import jax.numpy as jnp
from jax import lax
from jax.experimental import pallas as pl
from jax.experimental.pallas import tpu as pltpu
from jax.sharding import PartitionSpec as P

BLOCK = 128
ITERS = 2
UNROLL = 16
PARTS = 2
PIVOTS = 8
MESH = pl.DeviceIdType.MESH
HIGHEST = lax.Precision.HIGHEST
f32 = jnp.float32
bf16 = jnp.bfloat16
i32 = jnp.int32


def dot(left, right, dims):
    return lax.dot_general(
        left, right, (dims, ((), ())), precision=HIGHEST, preferred_element_type=f32
    )


def pair_gram(left, right):
    return dot(left, right, ((1,), (1,)))


def left_t(coeffs, panel):
    return dot(coeffs, panel, ((0,), (0,)))


def gauss_jordan(right, matrix, frames):
    aug = jnp.concatenate([right, matrix], axis=1)
    tiles = [aug[i : i + 8] for i in range(0, frames, 8)]
    sub = lax.broadcasted_iota(i32, tiles[0].shape, 0)
    for j in range(0, frames, PIVOTS):
        at, home, first = frames + j, j // 8, j % 8
        cols = [
            [jnp.broadcast_to(t[:, at + p : at + p + 1], t.shape) for t in tiles]
            for p in range(PIVOTS)
        ]
        lead = [tiles[home][first + q : first + q + 1] for q in range(PIVOTS)]
        small = [
            [cols[p][home][first + q : first + q + 1] for p in range(PIVOTS)]
            for q in range(PIVOTS)
        ]
        for p in range(PIVOTS):
            inverse = 1.0 / small[p][p]
            lead[p] = lead[p] * inverse
            for z in range(p + 1, PIVOTS):
                small[p][z] = small[p][z] * inverse
            for q in range(PIVOTS):
                if q != p:
                    factor = small[q][p]
                    lead[q] = lead[q] - factor * lead[p]
                    for z in range(p + 1, PIVOTS):
                        small[q][z] = small[q][z] - factor * small[p][z]
        for i in range(len(tiles)):
            new = tiles[i]
            for p in range(PIVOTS):
                new = new - cols[p][i] * lead[p]
            if i == home:
                for q in range(PIVOTS):
                    new = jnp.where(sub == first + q, lead[q], new)
            tiles[i] = new
    return jnp.concatenate(tiles, axis=0)[:, :frames]


def flip(value, mask):
    out, bit = value, 1
    while bit <= mask:
        if mask & bit:
            out = out + bit - 2 * bit * lax.rem(lax.div(value, bit), 2)
        bit *= 2
    return out


def order_by(key_row, key, other, kb):
    ids_row = lax.broadcasted_iota(i32, (1, kb), 1)
    ids = lax.broadcasted_iota(i32, (kb, 1), 0)
    before = key_row * kb + ids_row < key * kb + ids
    rank = jnp.sum(jnp.where(before, 1, 0), axis=1, keepdims=True)
    lane = lax.broadcasted_iota(i32, (kb, BLOCK), 1)
    take = lambda mask, value: jnp.sum(jnp.where(mask, value, 0), axis=0, keepdims=True)
    hot = rank == lane
    keys = take(hot, key)
    previous = take(rank + 1 == lane, key)
    keep = jnp.where((keys == previous) & (lane[:1] > 0), 1, 0)
    ends = jnp.maximum(take(key <= lane, 1) - 1, 0)
    valid = jnp.minimum(take(key == lane, 1), 1)
    return [take(hot, ids), take(hot, other), ends], [keep, valid]


def kernel(
    nr, nc, cb, kb, frames,
    rowi_hbm, coli_hbm, rhs_hbm, prior_hbm, blocks_hbm, sol_ref, res_ref,
    rowi, coli, tabv, keepv, tab, keep, rhs_ref, prior_ref,
    blocks, turned, panels, feet, csend, cland, xsend, xland, pair, sendb, landb, scan,
    image, direct, resid, foot, adjust,
    gca, gra, gcb, grb, gcc, grk,
    in_sem, tab_sem, ag_s, ag_r, ch_s, ch_r, xh_s, xh_r, fg_s, fg_r, br_s, br_r,
    ga_s, ga_r, gb_s, gb_r, gcb_s, gcb_r, grb_s, grb_r, gcc_s, gcc_r, gk_s, gk_r,
):
    r = lax.axis_index("row")
    c = lax.axis_index("col")
    nrow, ncol = cb * nc, cb * nr
    nx = nc // 2
    hrow = nrow // 2
    half = frames // 2
    part = frames // PARTS
    side = lax.rem(lax.rem(c, 2) + lax.div(c, 2), 2)
    span = lambda h: slice(h * part, (h + 1) * part)
    pending = []

    pairs = (
        (rhs_hbm, rhs_ref), (rowi_hbm, rowi), (coli_hbm, coli), (prior_hbm, prior_ref),
        (blocks_hbm, blocks),
    )
    loads = [
        pltpu.make_async_copy(src, dst, in_sem.at[i]) for i, (src, dst) in enumerate(pairs)
    ]
    for load in loads:
        load.start()

    barrier = pltpu.get_barrier_semaphore()
    for axis, me, n in (("row", r, nr), ("col", c, nc)):
        for m in range(n - 1, 0, -1):
            pl.semaphore_signal(
                barrier, inc=1, device_id={axis: flip(me, m)}, device_id_type=MESH
            )

    def push(axis, peer, src, dst, ssem, rsem):
        copy = pltpu.make_async_remote_copy(
            src_ref=src, dst_ref=dst, send_sem=ssem, recv_sem=rsem,
            device_id={axis: peer}, device_id_type=MESH,
        )
        copy.start()
        pending.append(copy)
        return copy

    def share(axis, me, n, buf, ssem, rsem, width=1):
        at = buf.at[pl.ds(me * width, width)]
        return [
            push(axis, flip(me, m), at, at, ssem.at[m - 1], rsem.at[m - 1])
            for m in range(n - 1, 0, -1)
        ]

    def arrive(copies):
        for copy in copies:
            copy.wait_recv()

    def total(buf, n):
        out = buf[0]
        for i in range(1, n):
            out = out + buf[i]
        return out

    def fold(gram):
        return jnp.concatenate([gram[:half], gram[half:]], axis=1)

    def unfold(packed):
        return jnp.concatenate([packed[:, :frames], packed[:, frames:]], axis=0)

    def put_panel(it, value):
        for h in range(PARTS):
            for b in range(cb):
                piece = value[span(h), b * BLOCK : (b + 1) * BLOCK]
                panels[h][it, r * cb + b] = piece.astype(bf16)

    def gather_rows(it):
        return [
            share("row", r, nr, panels[h].at[it], ag_s.at[it, h], ag_r.at[it, h], cb)
            for h in range(PARTS)
        ]

    def sweep(source, it, h, weight, pick, flags):
        def body(q, run):
            for u in range(UNROLL):
                t = q * UNROLL + u
                run = run * keep[flags, t] + lax.dot_general(
                    source[it, tab[pick, t]], weight(t), (((1,), (0,)), ((), ())),
                    preferred_element_type=f32,
                )
                scan[h, t] = run
            return run

        lax.fori_loop(0, kb // UNROLL, body, jnp.zeros((part, BLOCK), f32))

    def forward(it, h):
        sweep(panels[h], it, h, lambda t: turned[t], 1, 0)

    def backward(it, h):
        sweep(feet[h], it, h, lambda t: blocks[tab[3, t]], 4, 2)

    def segment(h, end_at, valid_at, i):
        return scan[h, tab[end_at, i]] * keep[valid_at, i]

    loads[0].wait()
    put_panel(0, rhs_ref[...])
    loads[1].wait()
    loads[2].wait()
    eye = lax.broadcasted_iota(i32, (kb, kb), 0) == lax.broadcasted_iota(i32, (kb, kb), 1)
    stand = lambda row: jnp.sum(jnp.where(eye, row, 0), axis=1, keepdims=True)
    bi, bj = rowi[...], coli[...]
    row_key = lax.rem(bi, nrow)
    col_key = lax.div(bj, nrow) * cb + lax.rem(bj, cb)
    row_up, col_up = stand(row_key), stand(col_key)
    ints_r, flags_r = order_by(row_key, row_up, col_up, kb)
    ints_c, flags_c = order_by(col_key, col_up, row_up, kb)
    blank = [jnp.zeros((1, BLOCK), i32)]
    tabv[...] = jnp.concatenate(ints_r + ints_c + blank * 2, axis=0)
    keepv[...] = jnp.concatenate(flags_r + flags_c + blank * 4, axis=0).astype(f32)
    tables = [
        pltpu.make_async_copy(tabv, tab, tab_sem.at[0]),
        pltpu.make_async_copy(keepv, keep, tab_sem.at[1]),
    ]
    for copy in tables:
        copy.start()
    loads[3].wait()
    rhs = rhs_ref[...]
    gca[c, :, :frames] = pair_gram(rhs, rhs)
    gca[c, :, frames:] = pair_gram(rhs, prior_ref[...] * rhs)
    pl.semaphore_wait(barrier, nr + nc - 2)

    gather = gather_rows(0)
    gram_cols = share("col", c, nc, gca, ga_s, ga_r)
    for copy in tables:
        copy.wait()
    loads[4].wait()

    def turn(q, _):
        for u in range(UNROLL):
            t = q * UNROLL + u
            turned[t] = blocks[tab[0, t]].T
        return 0

    lax.fori_loop(0, kb // UNROLL, turn, 0)
    arrive(gram_cols)
    sums = total(gca, nc)
    gra[r] = fold(sums[:, :frames])
    weighted = fold(sums[:, frames:])
    gram_rows = share("row", r, nr, gra, gb_s, gb_r)
    gram = inverse = alpha = None

    for it in range(ITERS):
        last = it + 1 == ITERS
        if it > 0:
            arrive(gram_cols)
            grb[it - 1, r] = total(gcb.at[it - 1], nc)
            gram_rows = share(
                "row", r, nr, grb.at[it - 1], grb_s.at[it - 1], grb_r.at[it - 1]
            )
        crossed = []
        for h in range(PARTS):
            arrive(gather[h])
            forward(it, h)
            for j in range(hrow):
                csend[it, h, j] = segment(h, 2, 1, (1 - side) * hrow + j)
            swapped = push(
                "col", flip(c, 1), csend.at[it, h], cland.at[it, h],
                ch_s.at[it, h], ch_r.at[it, h],
            )
            arrive([swapped])
            for j in range(hrow):
                own = segment(h, 2, 1, side * hrow + j) + cland[it, h, j]
                pair[h, j] = own
                xsend[it, h, j] = own.astype(bf16)
            crossed.append([
                push(
                    "col", flip(c, 2 * m + m % 2), xsend.at[it, h], xland.at[it, h, m - 1],
                    xh_s.at[it, h, m - 1], xh_r.at[it, h, m - 1],
                )
                for m in range(nx - 1, 0, -1)
            ])
        if it > 0:
            arrive(gram_rows)
            gram = unfold(total(grb.at[it - 1], nr))
            beta = dot(inverse, gram, ((1,), (0,)))
            adjust[...] = left_t(beta, foot[...])
            before = (rhs_ref if it == 1 else direct)[...]
            direct[...] = resid[...] + left_t(beta, before)
            direction = direct[...]
            gcc[it - 1, c] = fold(pair_gram(direction, prior_ref[...] * direction))
            weight_cols = share(
                "col", c, nc, gcc.at[it - 1], gcc_s.at[it - 1], gcc_r.at[it - 1]
            )
        spread = []
        for h in range(PARTS):
            arrive(crossed[h])
            for j in range(hrow):
                at = slice(j * BLOCK, (j + 1) * BLOCK)
                own = pair[h, j]
                for m in range(nx - 1):
                    own = own + xland[it, h, m, j].astype(f32)
                if it > 0:
                    own = own + adjust[span(h), at]
                if not last:
                    foot[span(h), at] = own
                feet[h][it, side * hrow + j] = own.astype(bf16)
            at = feet[h].at[it, pl.ds(side * hrow, hrow)]
            spread.append(push(
                "col", flip(c, 1), at, at, fg_s.at[it, h], fg_r.at[it, h]
            ))
        copies = []
        for h in range(PARTS):
            arrive([spread[h]])
            if h + 1 == PARTS:
                wide = jnp.concatenate(
                    [
                        jnp.concatenate([feet[p][it, i] for p in range(PARTS)], axis=0)
                        for i in range(nrow)
                    ],
                    axis=1,
                )
                square = lax.dot_general(
                    wide, wide, (((1,), (1,)), ((), ())), preferred_element_type=f32
                )
                if it > 0:
                    arrive(weight_cols)
                    weighted = total(gcc.at[it - 1], nc)
                grk[it, r] = fold(square) + weighted
                curve_rows = share("row", r, nr, grk.at[it], gk_s.at[it], gk_r.at[it])
            backward(it, h)
            for i in range(ncol):
                sendb[it, h, i] = segment(h, 5, 3, i).astype(bf16)
            copies.append([
                push(
                    "row", flip(r, m), sendb.at[it, h, pl.ds(flip(r, m) * cb, cb)],
                    landb.at[it, h, m - 1], br_s.at[it, h, m - 1], br_r.at[it, h, m - 1],
                )
                for m in range(nr - 1, 0, -1)
            ])
        if it == 0:
            arrive(gram_rows)
            gram = unfold(total(gra, nr))
        if not last:
            square = (frames, frames)
            ones = lax.broadcasted_iota(i32, square, 0) == lax.broadcasted_iota(i32, square, 1)
            inverse = gauss_jordan(jnp.where(ones, 1.0, 0.0), gram, frames)
        arrive(curve_rows)
        alpha = gauss_jordan(gram, unfold(total(grk.at[it], nr)), frames)
        now = rhs_ref if it == 0 else direct
        if last:
            update = left_t(alpha, now[...])
            sol_ref[...] = update if it == 0 else sol_ref[...] + update
        residual = (rhs_ref if it == 0 else resid)[...]
        for h in range(PARTS):
            arrive(copies[h])
            for b in range(cb):
                at = slice(b * BLOCK, (b + 1) * BLOCK)
                own = segment(h, 5, 3, r * cb + b)
                for o in range(nr - 1):
                    own = own + landb[it, h, o, b].astype(f32)
                image[span(h), at] = own + prior_ref[:, at] * now[span(h), at]
            residual = residual - left_t(alpha[span(h)], image[span(h), :])
        if last:
            res_ref[...] = residual
        else:
            put_panel(it + 1, residual)
            gather = gather_rows(it + 1)
            resid[...] = residual
            gcb[it, c] = fold(pair_gram(residual, residual))
            gram_cols = share("col", c, nc, gcb.at[it], gcb_s.at[it], gcb_r.at[it])
            update = left_t(alpha, now[...])
            sol_ref[...] = update if it == 0 else sol_ref[...] + update
    for copy in pending:
        copy.wait_send()


def shards(right_side, prior, blocks, block_row, block_col):
    frames, pix = right_side.shape
    kb = blocks.shape[0]
    cb = pix // BLOCK
    nr = lax.axis_size("row")
    nc = lax.axis_size("col")
    nrow, ncol = cb * nc, cb * nr
    hrow, nx = nrow // 2, nc // 2
    vm = pl.BlockSpec(memory_space=pltpu.VMEM)
    dma = pltpu.SemaphoreType.DMA
    tile = (frames // PARTS, BLOCK)
    pieces = (ITERS, PARTS)
    half = (frames // 2, 2 * frames)
    out = jax.ShapeDtypeStruct(right_side.shape, f32)
    return pl.pallas_call(
        functools.partial(kernel, nr, nc, cb, kb, frames),
        out_shape=(out, out),
        in_specs=[pl.BlockSpec(memory_space=pl.ANY)] * 5,
        out_specs=(vm, vm),
        scratch_shapes=[
            pltpu.VMEM((1, kb), i32),
            pltpu.VMEM((1, kb), i32),
            pltpu.VMEM((8, BLOCK), i32),
            pltpu.VMEM((8, BLOCK), f32),
            pltpu.SMEM((8, BLOCK), i32),
            pltpu.SMEM((8, BLOCK), f32),
            pltpu.VMEM(right_side.shape, f32),
            pltpu.VMEM((1, pix), f32),
            pltpu.VMEM(blocks.shape, bf16),
            pltpu.VMEM(blocks.shape, bf16),
            [pltpu.VMEM((ITERS, ncol) + tile, bf16)] * PARTS,
            [pltpu.VMEM((ITERS, nrow) + tile, bf16)] * PARTS,
            pltpu.VMEM(pieces + (hrow,) + tile, f32),
            pltpu.VMEM(pieces + (hrow,) + tile, f32),
            pltpu.VMEM(pieces + (hrow,) + tile, bf16),
            pltpu.VMEM(pieces + (nx - 1, hrow) + tile, bf16),
            pltpu.VMEM((PARTS, hrow) + tile, f32),
            pltpu.VMEM(pieces + (ncol,) + tile, bf16),
            pltpu.VMEM(pieces + (nr - 1, cb) + tile, bf16),
            pltpu.VMEM((PARTS, kb) + tile, f32),
            pltpu.VMEM(right_side.shape, f32),
            pltpu.VMEM(right_side.shape, f32),
            pltpu.VMEM(right_side.shape, f32),
            pltpu.VMEM((frames, hrow * BLOCK), f32),
            pltpu.VMEM((frames, hrow * BLOCK), f32),
            pltpu.VMEM((nc, frames, 2 * frames), f32),
            pltpu.VMEM((nr,) + half, f32),
            pltpu.VMEM((ITERS - 1, nc) + half, f32),
            pltpu.VMEM((ITERS - 1, nr) + half, f32),
            pltpu.VMEM((ITERS - 1, nc) + half, f32),
            pltpu.VMEM((ITERS, nr) + half, f32),
            dma((5,)),
            dma((2,)),
            dma(pieces + (nr - 1,)), dma(pieces + (nr - 1,)),
            dma(pieces), dma(pieces),
            dma(pieces + (nx - 1,)), dma(pieces + (nx - 1,)),
            dma(pieces), dma(pieces),
            dma(pieces + (nr - 1,)), dma(pieces + (nr - 1,)),
            dma((nc - 1,)), dma((nc - 1,)),
            dma((nr - 1,)), dma((nr - 1,)),
            dma((ITERS - 1, nc - 1)), dma((ITERS - 1, nc - 1)),
            dma((ITERS - 1, nr - 1)), dma((ITERS - 1, nr - 1)),
            dma((ITERS - 1, nc - 1)), dma((ITERS - 1, nc - 1)),
            dma((ITERS, nr - 1)), dma((ITERS, nr - 1)),
        ],
        compiler_params=pltpu.CompilerParams(
            collective_id=0, has_side_effects=True, vmem_limit_bytes=60 << 20
        ),
    )(block_row[None, :], block_col[None, :], right_side, prior[None, :], blocks)


def solution(mesh):
    return jax.shard_map(
        shards,
        mesh=mesh,
        in_specs=(
            P("groups", ("row", "col")),
            P(("row", "col")),
            P(("row", "col"), None, None),
            P(("row", "col")),
            P(("row", "col")),
        ),
        out_specs=(P("groups", ("row", "col")), P("groups", ("row", "col"))),
        check_vma=False,
    )
```

```python
import functools

import jax
import jax.numpy as jnp
from jax import lax
from jax.experimental import pallas as pl
from jax.experimental.pallas import tpu as pltpu
from jax.sharding import PartitionSpec as P

BLOCK = 128
ITERS = 2
UNROLL = 16
PARTS = 2
PIVOTS = 8
MESH = pl.DeviceIdType.MESH
HIGHEST = lax.Precision.HIGHEST
f32 = jnp.float32
bf16 = jnp.bfloat16
i32 = jnp.int32


def dot(left, right, dims):
    return lax.dot_general(
        left, right, (dims, ((), ())), precision=HIGHEST, preferred_element_type=f32
    )


def pair_gram(left, right):
    return dot(left, right, ((1,), (1,)))


def left_t(coeffs, panel):
    return dot(coeffs, panel, ((0,), (0,)))


def gauss_jordan(right, matrix, frames):
    aug = jnp.concatenate([right, matrix], axis=1)
    tiles = [aug[i : i + 8] for i in range(0, frames, 8)]
    sub = lax.broadcasted_iota(i32, tiles[0].shape, 0)
    for j in range(0, frames, PIVOTS):
        at, home, first = frames + j, j // 8, j % 8
        cols = [
            [jnp.broadcast_to(t[:, at + p : at + p + 1], t.shape) for t in tiles]
            for p in range(PIVOTS)
        ]
        lead = [tiles[home][first + q : first + q + 1] for q in range(PIVOTS)]
        small = [
            [cols[p][home][first + q : first + q + 1] for p in range(PIVOTS)]
            for q in range(PIVOTS)
        ]
        for p in range(PIVOTS):
            inverse = 1.0 / small[p][p]
            lead[p] = lead[p] * inverse
            for z in range(p + 1, PIVOTS):
                small[p][z] = small[p][z] * inverse
            for q in range(PIVOTS):
                if q != p:
                    factor = small[q][p]
                    lead[q] = lead[q] - factor * lead[p]
                    for z in range(p + 1, PIVOTS):
                        small[q][z] = small[q][z] - factor * small[p][z]
        for i in range(len(tiles)):
            new = tiles[i]
            for p in range(PIVOTS):
                new = new - cols[p][i] * lead[p]
            if i == home:
                for q in range(PIVOTS):
                    new = jnp.where(sub == first + q, lead[q], new)
            tiles[i] = new
    return jnp.concatenate(tiles, axis=0)[:, :frames]


def flip(value, mask):
    out, bit = value, 1
    while bit <= mask:
        if mask & bit:
            out = out + bit - 2 * bit * lax.rem(lax.div(value, bit), 2)
        bit *= 2
    return out


def order_by(key_row, key, other, kb):
    ids_row = lax.broadcasted_iota(i32, (1, kb), 1)
    ids = lax.broadcasted_iota(i32, (kb, 1), 0)
    before = key_row * kb + ids_row < key * kb + ids
    rank = jnp.sum(jnp.where(before, 1, 0), axis=1, keepdims=True)
    lane = lax.broadcasted_iota(i32, (kb, BLOCK), 1)
    take = lambda mask, value: jnp.sum(jnp.where(mask, value, 0), axis=0, keepdims=True)
    hot = rank == lane
    keys = take(hot, key)
    previous = take(rank + 1 == lane, key)
    keep = jnp.where((keys == previous) & (lane[:1] > 0), 1, 0)
    ends = jnp.maximum(take(key <= lane, 1) - 1, 0)
    valid = jnp.minimum(take(key == lane, 1), 1)
    return [take(hot, ids), take(hot, other), ends], [keep, valid]


def kernel(
    nr, nc, cb, kb, frames,
    rowi_hbm, coli_hbm, rhs_hbm, prior_hbm, blocks_hbm, sol_ref, res_ref,
    rowi, coli, tabv, keepv, tab, keep, rhs_ref, prior_ref,
    blocks, turned, panels, feet, csend, cland, xsend, xland, pair, sendb, landb, scan,
    image, direct, resid, foot, adjust,
    gca, gra, gcb, grb, gcc, grk,
    in_sem, tab_sem, ag_s, ag_r, ch_s, ch_r, xh_s, xh_r, fg_s, fg_r, br_s, br_r,
    ga_s, ga_r, gb_s, gb_r, gcb_s, gcb_r, grb_s, grb_r, gcc_s, gcc_r, gk_s, gk_r,
):
    r = lax.axis_index("row")
    c = lax.axis_index("col")
    nrow, ncol = cb * nc, cb * nr
    nx = nc // 2
    hrow = nrow // 2
    half = frames // 2
    part = frames // PARTS
    side = lax.rem(lax.rem(c, 2) + lax.div(c, 2), 2)
    span = lambda h: slice(h * part, (h + 1) * part)
    pending = []

    pairs = (
        (rhs_hbm, rhs_ref), (rowi_hbm, rowi), (coli_hbm, coli), (prior_hbm, prior_ref),
        (blocks_hbm, blocks),
    )
    loads = [
        pltpu.make_async_copy(src, dst, in_sem.at[i]) for i, (src, dst) in enumerate(pairs)
    ]
    for load in loads:
        load.start()

    barrier = pltpu.get_barrier_semaphore()
    for axis, me, n in (("row", r, nr), ("col", c, nc)):
        for m in range(n - 1, 0, -1):
            pl.semaphore_signal(
                barrier, inc=1, device_id={axis: flip(me, m)}, device_id_type=MESH
            )

    def push(axis, peer, src, dst, ssem, rsem):
        copy = pltpu.make_async_remote_copy(
            src_ref=src, dst_ref=dst, send_sem=ssem, recv_sem=rsem,
            device_id={axis: peer}, device_id_type=MESH,
        )
        copy.start()
        pending.append(copy)
        return copy

    def share(axis, me, n, buf, ssem, rsem, width=1):
        at = buf.at[pl.ds(me * width, width)]
        return [
            push(axis, flip(me, m), at, at, ssem.at[m - 1], rsem.at[m - 1])
            for m in range(n - 1, 0, -1)
        ]

    def arrive(copies):
        for copy in copies:
            copy.wait_recv()

    def total(buf, n):
        out = buf[0]
        for i in range(1, n):
            out = out + buf[i]
        return out

    def fold(gram):
        return jnp.concatenate([gram[:half], gram[half:]], axis=1)

    def unfold(packed):
        return jnp.concatenate([packed[:, :frames], packed[:, frames:]], axis=0)

    def put_panel(it, value):
        for h in range(PARTS):
            for b in range(cb):
                piece = value[span(h), b * BLOCK : (b + 1) * BLOCK]
                panels[h][it, r * cb + b] = piece.astype(bf16)

    def gather_rows(it):
        return [
            share("row", r, nr, panels[h].at[it], ag_s.at[it, h], ag_r.at[it, h], cb)
            for h in range(PARTS)
        ]

    def sweep(source, it, h, weight, pick, flags):
        def body(q, run):
            for u in range(UNROLL):
                t = q * UNROLL + u
                run = run * keep[flags, t] + lax.dot_general(
                    source[it, tab[pick, t]], weight(t), (((1,), (0,)), ((), ())),
                    preferred_element_type=f32,
                )
                scan[h, t] = run
            return run

        lax.fori_loop(0, kb // UNROLL, body, jnp.zeros((part, BLOCK), f32))

    def forward(it, h):
        sweep(panels[h], it, h, lambda t: turned[t], 1, 0)

    def backward(it, h):
        sweep(feet[h], it, h, lambda t: blocks[tab[3, t]], 4, 2)

    def segment(h, end_at, valid_at, i):
        return scan[h, tab[end_at, i]] * keep[valid_at, i]

    loads[0].wait()
    put_panel(0, rhs_ref[...])
    loads[1].wait()
    loads[2].wait()
    eye = lax.broadcasted_iota(i32, (kb, kb), 0) == lax.broadcasted_iota(i32, (kb, kb), 1)
    stand = lambda row: jnp.sum(jnp.where(eye, row, 0), axis=1, keepdims=True)
    bi, bj = rowi[...], coli[...]
    row_key = lax.rem(bi, nrow)
    col_key = lax.div(bj, nrow) * cb + lax.rem(bj, cb)
    row_up, col_up = stand(row_key), stand(col_key)
    ints_r, flags_r = order_by(row_key, row_up, col_up, kb)
    ints_c, flags_c = order_by(col_key, col_up, row_up, kb)
    blank = [jnp.zeros((1, BLOCK), i32)]
    tabv[...] = jnp.concatenate(ints_r + ints_c + blank * 2, axis=0)
    keepv[...] = jnp.concatenate(flags_r + flags_c + blank * 4, axis=0).astype(f32)
    tables = [
        pltpu.make_async_copy(tabv, tab, tab_sem.at[0]),
        pltpu.make_async_copy(keepv, keep, tab_sem.at[1]),
    ]
    for copy in tables:
        copy.start()
    loads[3].wait()
    rhs = rhs_ref[...]
    gca[c, :, :frames] = pair_gram(rhs, rhs)
    gca[c, :, frames:] = pair_gram(rhs, prior_ref[...] * rhs)
    pl.semaphore_wait(barrier, nr + nc - 2)

    gather = gather_rows(0)
    gram_cols = share("col", c, nc, gca, ga_s, ga_r)
    for copy in tables:
        copy.wait()
    loads[4].wait()

    def turn(q, _):
        for u in range(UNROLL):
            t = q * UNROLL + u
            turned[t] = blocks[tab[0, t]].T
        return 0

    lax.fori_loop(0, kb // UNROLL, turn, 0)
    arrive(gram_cols)
    sums = total(gca, nc)
    gra[r] = fold(sums[:, :frames])
    weighted = fold(sums[:, frames:])
    gram_rows = share("row", r, nr, gra, gb_s, gb_r)
    gram = inverse = alpha = None

    for it in range(ITERS):
        last = it + 1 == ITERS
        if it > 0:
            arrive(gram_cols)
            grb[it - 1, r] = total(gcb.at[it - 1], nc)
            gram_rows = share(
                "row", r, nr, grb.at[it - 1], grb_s.at[it - 1], grb_r.at[it - 1]
            )
        crossed = []
        for h in range(PARTS):
            arrive(gather[h])
            forward(it, h)
            for j in range(hrow):
                csend[it, h, j] = segment(h, 2, 1, (1 - side) * hrow + j)
            swapped = push(
                "col", flip(c, 1), csend.at[it, h], cland.at[it, h],
                ch_s.at[it, h], ch_r.at[it, h],
            )
            arrive([swapped])
            for j in range(hrow):
                own = segment(h, 2, 1, side * hrow + j) + cland[it, h, j]
                pair[h, j] = own
                xsend[it, h, j] = own.astype(bf16)
            crossed.append([
                push(
                    "col", flip(c, 2 * m + m % 2), xsend.at[it, h], xland.at[it, h, m - 1],
                    xh_s.at[it, h, m - 1], xh_r.at[it, h, m - 1],
                )
                for m in range(nx - 1, 0, -1)
            ])
        if it > 0:
            arrive(gram_rows)
            gram = unfold(total(grb.at[it - 1], nr))
            beta = dot(inverse, gram, ((1,), (0,)))
            adjust[...] = left_t(beta, foot[...])
            before = (rhs_ref if it == 1 else direct)[...]
            direct[...] = resid[...] + left_t(beta, before)
            direction = direct[...]
            gcc[it - 1, c] = fold(pair_gram(direction, prior_ref[...] * direction))
            weight_cols = share(
                "col", c, nc, gcc.at[it - 1], gcc_s.at[it - 1], gcc_r.at[it - 1]
            )
        spread = []
        for h in range(PARTS):
            arrive(crossed[h])
            for j in range(hrow):
                at = slice(j * BLOCK, (j + 1) * BLOCK)
                own = pair[h, j]
                for m in range(nx - 1):
                    own = own + xland[it, h, m, j].astype(f32)
                if it > 0:
                    own = own + adjust[span(h), at]
                if not last:
                    foot[span(h), at] = own
                feet[h][it, side * hrow + j] = own.astype(bf16)
            at = feet[h].at[it, pl.ds(side * hrow, hrow)]
            spread.append(push(
                "col", flip(c, 1), at, at, fg_s.at[it, h], fg_r.at[it, h]
            ))
        copies = []
        for h in range(PARTS):
            arrive([spread[h]])
            if h + 1 == PARTS:
                wide = jnp.concatenate(
                    [
                        jnp.concatenate([feet[p][it, i] for p in range(PARTS)], axis=0)
                        for i in range(nrow)
                    ],
                    axis=1,
                )
                square = lax.dot_general(
                    wide, wide, (((1,), (1,)), ((), ())), preferred_element_type=f32
                )
                if it > 0:
                    arrive(weight_cols)
                    weighted = total(gcc.at[it - 1], nc)
                grk[it, r] = fold(square) + weighted
                curve_rows = share("row", r, nr, grk.at[it], gk_s.at[it], gk_r.at[it])
            backward(it, h)
            for i in range(ncol):
                sendb[it, h, i] = segment(h, 5, 3, i).astype(bf16)
            copies.append([
                push(
                    "row", flip(r, m), sendb.at[it, h, pl.ds(flip(r, m) * cb, cb)],
                    landb.at[it, h, m - 1], br_s.at[it, h, m - 1], br_r.at[it, h, m - 1],
                )
                for m in range(nr - 1, 0, -1)
            ])
        if it == 0:
            arrive(gram_rows)
            gram = unfold(total(gra, nr))
        if not last:
            square = (frames, frames)
            ones = lax.broadcasted_iota(i32, square, 0) == lax.broadcasted_iota(i32, square, 1)
            inverse = gauss_jordan(jnp.where(ones, 1.0, 0.0), gram, frames)
        arrive(curve_rows)
        alpha = gauss_jordan(gram, unfold(total(grk.at[it], nr)), frames)
        now = rhs_ref if it == 0 else direct
        if last:
            update = left_t(alpha, now[...])
            sol_ref[...] = update if it == 0 else sol_ref[...] + update
        residual = (rhs_ref if it == 0 else resid)[...]
        for h in range(PARTS):
            arrive(copies[h])
            for b in range(cb):
                at = slice(b * BLOCK, (b + 1) * BLOCK)
                own = segment(h, 5, 3, r * cb + b)
                for o in range(nr - 1):
                    own = own + landb[it, h, o, b].astype(f32)
                image[span(h), at] = own + prior_ref[:, at] * now[span(h), at]
            residual = residual - left_t(alpha[span(h)], image[span(h), :])
        if last:
            res_ref[...] = residual
        else:
            put_panel(it + 1, residual)
            gather = gather_rows(it + 1)
            resid[...] = residual
            gcb[it, c] = fold(pair_gram(residual, residual))
            gram_cols = share("col", c, nc, gcb.at[it], gcb_s.at[it], gcb_r.at[it])
            update = left_t(alpha, now[...])
            sol_ref[...] = update if it == 0 else sol_ref[...] + update
    for copy in pending:
        copy.wait_send()


def store(sol, res, sol_hbm, res_hbm, sem):
    copies = [
        pltpu.make_async_copy(src, dst, sem.at[i])
        for i, (src, dst) in enumerate(((sol, sol_hbm), (res, res_hbm)))
    ]
    for copy in copies:
        copy.start()
    for copy in copies:
        copy.wait()


def in_hbm(array):
    return pltpu.with_memory_space_constraint(array, pltpu.HBM)


def shards(right_side, prior, blocks, block_row, block_col):
    frames, pix = right_side.shape
    kb = blocks.shape[0]
    cb = pix // BLOCK
    nr = lax.axis_size("row")
    nc = lax.axis_size("col")
    nrow, ncol = cb * nc, cb * nr
    hrow, nx = nrow // 2, nc // 2
    vm = pl.BlockSpec(memory_space=pltpu.VMEM)
    dma = pltpu.SemaphoreType.DMA
    tile = (frames // PARTS, BLOCK)
    pieces = (ITERS, PARTS)
    half = (frames // 2, 2 * frames)
    out = jax.ShapeDtypeStruct(right_side.shape, f32)
    made = pl.pallas_call(
        functools.partial(kernel, nr, nc, cb, kb, frames),
        out_shape=(out, out),
        in_specs=[pl.BlockSpec(memory_space=pltpu.HBM)] * 5,
        out_specs=(vm, vm),
        scratch_shapes=[
            pltpu.VMEM((1, kb), i32),
            pltpu.VMEM((1, kb), i32),
            pltpu.VMEM((8, BLOCK), i32),
            pltpu.VMEM((8, BLOCK), f32),
            pltpu.SMEM((8, BLOCK), i32),
            pltpu.SMEM((8, BLOCK), f32),
            pltpu.VMEM(right_side.shape, f32),
            pltpu.VMEM((1, pix), f32),
            pltpu.VMEM(blocks.shape, bf16),
            pltpu.VMEM(blocks.shape, bf16),
            [pltpu.VMEM((ITERS, ncol) + tile, bf16)] * PARTS,
            [pltpu.VMEM((ITERS, nrow) + tile, bf16)] * PARTS,
            pltpu.VMEM(pieces + (hrow,) + tile, f32),
            pltpu.VMEM(pieces + (hrow,) + tile, f32),
            pltpu.VMEM(pieces + (hrow,) + tile, bf16),
            pltpu.VMEM(pieces + (nx - 1, hrow) + tile, bf16),
            pltpu.VMEM((PARTS, hrow) + tile, f32),
            pltpu.VMEM(pieces + (ncol,) + tile, bf16),
            pltpu.VMEM(pieces + (nr - 1, cb) + tile, bf16),
            pltpu.VMEM((PARTS, kb) + tile, f32),
            pltpu.VMEM(right_side.shape, f32),
            pltpu.VMEM(right_side.shape, f32),
            pltpu.VMEM(right_side.shape, f32),
            pltpu.VMEM((frames, hrow * BLOCK), f32),
            pltpu.VMEM((frames, hrow * BLOCK), f32),
            pltpu.VMEM((nc, frames, 2 * frames), f32),
            pltpu.VMEM((nr,) + half, f32),
            pltpu.VMEM((ITERS - 1, nc) + half, f32),
            pltpu.VMEM((ITERS - 1, nr) + half, f32),
            pltpu.VMEM((ITERS - 1, nc) + half, f32),
            pltpu.VMEM((ITERS, nr) + half, f32),
            dma((5,)),
            dma((2,)),
            dma(pieces + (nr - 1,)), dma(pieces + (nr - 1,)),
            dma(pieces), dma(pieces),
            dma(pieces + (nx - 1,)), dma(pieces + (nx - 1,)),
            dma(pieces), dma(pieces),
            dma(pieces + (nr - 1,)), dma(pieces + (nr - 1,)),
            dma((nc - 1,)), dma((nc - 1,)),
            dma((nr - 1,)), dma((nr - 1,)),
            dma((ITERS - 1, nc - 1)), dma((ITERS - 1, nc - 1)),
            dma((ITERS - 1, nr - 1)), dma((ITERS - 1, nr - 1)),
            dma((ITERS - 1, nc - 1)), dma((ITERS - 1, nc - 1)),
            dma((ITERS, nr - 1)), dma((ITERS, nr - 1)),
        ],
        compiler_params=pltpu.CompilerParams(
            collective_id=0, has_side_effects=True, vmem_limit_bytes=32 << 20
        ),
    )(*map(in_hbm, (block_row[None, :], block_col[None, :], right_side, prior[None, :], blocks)))
    return pl.pallas_call(
        store,
        out_shape=(out, out),
        in_specs=[pl.BlockSpec(memory_space=pl.ANY)] * 2,
        out_specs=(pl.BlockSpec(memory_space=pltpu.HBM),) * 2,
        scratch_shapes=[dma((2,))],
        compiler_params=pltpu.CompilerParams(vmem_limit_bytes=1 << 20),
    )(*made)


def solution(mesh):
    return jax.shard_map(
        shards,
        mesh=mesh,
        in_specs=(
            P("groups", ("row", "col")),
            P(("row", "col")),
            P(("row", "col"), None, None),
            P(("row", "col")),
            P(("row", "col")),
        ),
        out_specs=(P("groups", ("row", "col")), P("groups", ("row", "col"))),
        check_vma=False,
    )
```

```python
import functools

import jax
import jax.numpy as jnp
from jax import lax
from jax.experimental import pallas as pl
from jax.experimental.pallas import tpu as pltpu
from jax.sharding import PartitionSpec as P

BLOCK = 128
ITERS = 2
UNROLL = 64
PARTS = 2
PIVOTS = 8
MESH = pl.DeviceIdType.MESH
HIGHEST = lax.Precision.HIGHEST
f32 = jnp.float32
bf16 = jnp.bfloat16
i32 = jnp.int32


def dot(left, right, dims):
    return lax.dot_general(
        left, right, (dims, ((), ())), precision=HIGHEST, preferred_element_type=f32
    )


def pair_gram(left, right):
    return dot(left, right, ((1,), (1,)))


def left_t(coeffs, panel):
    return dot(coeffs, panel, ((0,), (0,)))


def gauss_jordan(right, matrix, frames):
    aug = jnp.concatenate([right, matrix], axis=1)
    tiles = [aug[i : i + 8] for i in range(0, frames, 8)]
    sub = lax.broadcasted_iota(i32, tiles[0].shape, 0)
    for j in range(0, frames, PIVOTS):
        at, home, first = frames + j, j // 8, j % 8
        cols = [
            [jnp.broadcast_to(t[:, at + p : at + p + 1], t.shape) for t in tiles]
            for p in range(PIVOTS)
        ]
        lead = [tiles[home][first + q : first + q + 1] for q in range(PIVOTS)]
        small = [
            [cols[p][home][first + q : first + q + 1] for p in range(PIVOTS)]
            for q in range(PIVOTS)
        ]
        for p in range(PIVOTS):
            inverse = 1.0 / small[p][p]
            lead[p] = lead[p] * inverse
            for z in range(p + 1, PIVOTS):
                small[p][z] = small[p][z] * inverse
            for q in range(PIVOTS):
                if q != p:
                    factor = small[q][p]
                    lead[q] = lead[q] - factor * lead[p]
                    for z in range(p + 1, PIVOTS):
                        small[q][z] = small[q][z] - factor * small[p][z]
        for i in range(len(tiles)):
            new = tiles[i]
            for p in range(PIVOTS):
                new = new - cols[p][i] * lead[p]
            if i == home:
                for q in range(PIVOTS):
                    new = jnp.where(sub == first + q, lead[q], new)
            tiles[i] = new
    return jnp.concatenate(tiles, axis=0)[:, :frames]


def flip(value, mask):
    out, bit = value, 1
    while bit <= mask:
        if mask & bit:
            out = out + bit - 2 * bit * lax.rem(lax.div(value, bit), 2)
        bit *= 2
    return out


def order_by(key_row, key, other, kb):
    ids_row = lax.broadcasted_iota(i32, (1, kb), 1)
    ids = lax.broadcasted_iota(i32, (kb, 1), 0)
    before = key_row * kb + ids_row < key * kb + ids
    rank = jnp.sum(jnp.where(before, 1, 0), axis=1, keepdims=True)
    lane = lax.broadcasted_iota(i32, (kb, BLOCK), 1)
    take = lambda mask, value: jnp.sum(jnp.where(mask, value, 0), axis=0, keepdims=True)
    hot = rank == lane
    keys = take(hot, key)
    previous = take(rank + 1 == lane, key)
    keep = jnp.where((keys == previous) & (lane[:1] > 0), 1, 0)
    ends = jnp.maximum(take(key <= lane, 1) - 1, 0)
    valid = jnp.minimum(take(key == lane, 1), 1)
    return [take(hot, ids), take(hot, other), ends], [keep, valid]


def kernel(
    nr, nc, cb, kb, frames,
    rowi_hbm, coli_hbm, rhs_hbm, prior_hbm, blocks_hbm, sol_ref, res_ref,
    rowi, coli, tabv, keepv, tab, keep, rhs_ref, prior_ref,
    blocks, turned, panels, feet, csend, cland, xsend, xland, pair, sendb, landb, scan,
    image, direct, resid, foot, adjust,
    gca, gra, gcb, grb, gcc, grk,
    in_sem, tab_sem, ag_s, ag_r, ch_s, ch_r, xh_s, xh_r, fg_s, fg_r, br_s, br_r,
    ga_s, ga_r, gb_s, gb_r, gcb_s, gcb_r, grb_s, grb_r, gcc_s, gcc_r, gk_s, gk_r,
):
    r = lax.axis_index("row")
    c = lax.axis_index("col")
    nrow, ncol = cb * nc, cb * nr
    nx = nc // 2
    hrow = nrow // 2
    half = frames // 2
    part = frames // PARTS
    side = lax.rem(lax.rem(c, 2) + lax.div(c, 2), 2)
    span = lambda h: slice(h * part, (h + 1) * part)
    pending = []

    pairs = (
        (rhs_hbm, rhs_ref), (rowi_hbm, rowi), (coli_hbm, coli), (prior_hbm, prior_ref),
        (blocks_hbm, blocks),
    )
    loads = [
        pltpu.make_async_copy(src, dst, in_sem.at[i]) for i, (src, dst) in enumerate(pairs)
    ]
    for load in loads:
        load.start()

    barrier = pltpu.get_barrier_semaphore()
    for axis, me, n in (("row", r, nr), ("col", c, nc)):
        for m in range(n - 1, 0, -1):
            pl.semaphore_signal(
                barrier, inc=1, device_id={axis: flip(me, m)}, device_id_type=MESH
            )

    def push(axis, peer, src, dst, ssem, rsem):
        copy = pltpu.make_async_remote_copy(
            src_ref=src, dst_ref=dst, send_sem=ssem, recv_sem=rsem,
            device_id={axis: peer}, device_id_type=MESH,
        )
        copy.start()
        pending.append(copy)
        return copy

    def share(axis, me, n, buf, ssem, rsem, width=1):
        at = buf.at[pl.ds(me * width, width)]
        return [
            push(axis, flip(me, m), at, at, ssem.at[m - 1], rsem.at[m - 1])
            for m in range(n - 1, 0, -1)
        ]

    def arrive(copies):
        for copy in copies:
            copy.wait_recv()

    def total(buf, n):
        out = buf[0]
        for i in range(1, n):
            out = out + buf[i]
        return out

    def fold(gram):
        return jnp.concatenate([gram[:half], gram[half:]], axis=1)

    def unfold(packed):
        return jnp.concatenate([packed[:, :frames], packed[:, frames:]], axis=0)

    def put_panel(it, value):
        for h in range(PARTS):
            for b in range(cb):
                piece = value[span(h), b * BLOCK : (b + 1) * BLOCK]
                panels[h][it, r * cb + b] = piece.astype(bf16)

    def gather_rows(it):
        return [
            share("row", r, nr, panels[h].at[it], ag_s.at[it, h], ag_r.at[it, h], cb)
            for h in range(PARTS)
        ]

    def sweep(source, it, h, weight, pick, flags):
        def body(q, run):
            for u in range(UNROLL):
                t = q * UNROLL + u
                run = run * keep[flags, t] + lax.dot_general(
                    source[it, tab[pick, t]], weight(t), (((1,), (0,)), ((), ())),
                    preferred_element_type=f32,
                )
                scan[h, t] = run
            return run

        lax.fori_loop(0, kb // UNROLL, body, jnp.zeros((part, BLOCK), f32))

    def forward(it, h):
        sweep(panels[h], it, h, lambda t: turned[t], 1, 0)

    def backward(it, h):
        sweep(feet[h], it, h, lambda t: blocks[tab[3, t]], 4, 2)

    def half_square(it, which):
        wide = jnp.concatenate(
            [
                jnp.concatenate(
                    [feet[p][it, which * hrow + j] for p in range(PARTS)], axis=0
                )
                for j in range(hrow)
            ],
            axis=1,
        )
        return lax.dot_general(
            wide, wide, (((1,), (1,)), ((), ())), preferred_element_type=f32
        )

    def segment(h, end_at, valid_at, i):
        return scan[h, tab[end_at, i]] * keep[valid_at, i]

    loads[0].wait()
    put_panel(0, rhs_ref[...])
    pl.semaphore_wait(barrier, nr + nc - 2)
    gather = gather_rows(0)
    loads[1].wait()
    loads[2].wait()
    eye = lax.broadcasted_iota(i32, (kb, kb), 0) == lax.broadcasted_iota(i32, (kb, kb), 1)
    stand = lambda row: jnp.sum(jnp.where(eye, row, 0), axis=1, keepdims=True)
    bi, bj = rowi[...], coli[...]
    row_key = lax.rem(bi, nrow)
    col_key = lax.div(bj, nrow) * cb + lax.rem(bj, cb)
    row_up, col_up = stand(row_key), stand(col_key)
    ints_r, flags_r = order_by(row_key, row_up, col_up, kb)
    ints_c, flags_c = order_by(col_key, col_up, row_up, kb)
    blank = [jnp.zeros((1, BLOCK), i32)]
    tabv[...] = jnp.concatenate(ints_r + ints_c + blank * 2, axis=0)
    keepv[...] = jnp.concatenate(flags_r + flags_c + blank * 4, axis=0).astype(f32)
    tables = [
        pltpu.make_async_copy(tabv, tab, tab_sem.at[0]),
        pltpu.make_async_copy(keepv, keep, tab_sem.at[1]),
    ]
    for copy in tables:
        copy.start()
    loads[3].wait()
    rhs = rhs_ref[...]
    gca[c, :, :frames] = pair_gram(rhs, rhs)
    gca[c, :, frames:] = pair_gram(rhs, prior_ref[...] * rhs)
    gram_cols = share("col", c, nc, gca, ga_s, ga_r)
    for copy in tables:
        copy.wait()
    loads[4].wait()

    def turn(q, _):
        for u in range(UNROLL):
            t = q * UNROLL + u
            turned[t] = blocks[tab[0, t]].T
        return 0

    lax.fori_loop(0, kb // UNROLL, turn, 0)
    arrive(gram_cols)
    sums = total(gca, nc)
    gra[r] = fold(sums[:, :frames])
    weighted = fold(sums[:, frames:])
    gram_rows = share("row", r, nr, gra, gb_s, gb_r)
    gram = inverse = alpha = None

    for it in range(ITERS):
        last = it + 1 == ITERS
        if it > 0:
            arrive(gram_cols)
            grb[it - 1, r] = total(gcb.at[it - 1], nc)
            gram_rows = share(
                "row", r, nr, grb.at[it - 1], grb_s.at[it - 1], grb_r.at[it - 1]
            )
        crossed = []
        for h in range(PARTS):
            arrive(gather[h])
            forward(it, h)
            for j in range(hrow):
                csend[it, h, j] = segment(h, 2, 1, (1 - side) * hrow + j)
            swapped = push(
                "col", flip(c, 1), csend.at[it, h], cland.at[it, h],
                ch_s.at[it, h], ch_r.at[it, h],
            )
            arrive([swapped])
            for j in range(hrow):
                own = segment(h, 2, 1, side * hrow + j) + cland[it, h, j]
                pair[h, j] = own
                xsend[it, h, j] = own.astype(bf16)
            crossed.append([
                push(
                    "col", flip(c, 2 * m + m % 2), xsend.at[it, h], xland.at[it, h, m - 1],
                    xh_s.at[it, h, m - 1], xh_r.at[it, h, m - 1],
                )
                for m in range(nx - 1, 0, -1)
            ])
        if it > 0:
            arrive(gram_rows)
            gram = unfold(total(grb.at[it - 1], nr))
            beta = dot(inverse, gram, ((1,), (0,)))
            adjust[...] = left_t(beta, foot[...])
            before = (rhs_ref if it == 1 else direct)[...]
            direct[...] = resid[...] + left_t(beta, before)
            direction = direct[...]
            gcc[it - 1, c] = fold(pair_gram(direction, prior_ref[...] * direction))
            weight_cols = share(
                "col", c, nc, gcc.at[it - 1], gcc_s.at[it - 1], gcc_r.at[it - 1]
            )
        copies = []
        for h in range(PARTS):
            arrive(crossed[h])
            for j in range(hrow):
                at = slice(j * BLOCK, (j + 1) * BLOCK)
                own = pair[h, j]
                for m in range(nx - 1):
                    own = own + xland[it, h, m, j].astype(f32)
                if it > 0:
                    own = own + adjust[span(h), at]
                if not last:
                    foot[span(h), at] = own
                feet[h][it, side * hrow + j] = own.astype(bf16)
            at = feet[h].at[it, pl.ds(side * hrow, hrow)]
            spread = push("col", flip(c, 1), at, at, fg_s.at[it, h], fg_r.at[it, h])
            if h + 1 == PARTS:
                square = half_square(it, side)
            arrive([spread])
            if h + 1 == PARTS:
                square = square + half_square(it, 1 - side)
                if it > 0:
                    arrive(weight_cols)
                    weighted = total(gcc.at[it - 1], nc)
                grk[it, r] = fold(square) + weighted
                curve_rows = share("row", r, nr, grk.at[it], gk_s.at[it], gk_r.at[it])
            backward(it, h)
            for i in range(ncol):
                sendb[it, h, i] = segment(h, 5, 3, i).astype(bf16)
            copies.append([
                push(
                    "row", flip(r, m), sendb.at[it, h, pl.ds(flip(r, m) * cb, cb)],
                    landb.at[it, h, m - 1], br_s.at[it, h, m - 1], br_r.at[it, h, m - 1],
                )
                for m in range(nr - 1, 0, -1)
            ])
        if it == 0:
            arrive(gram_rows)
            gram = unfold(total(gra, nr))
        if not last:
            square = (frames, frames)
            ones = lax.broadcasted_iota(i32, square, 0) == lax.broadcasted_iota(i32, square, 1)
            inverse = gauss_jordan(jnp.where(ones, 1.0, 0.0), gram, frames)
        arrive(curve_rows)
        alpha = gauss_jordan(gram, unfold(total(grk.at[it], nr)), frames)
        now = rhs_ref if it == 0 else direct
        if last:
            update = left_t(alpha, now[...])
            sol_ref[...] = update if it == 0 else sol_ref[...] + update
        residual = (rhs_ref if it == 0 else resid)[...]
        for h in range(PARTS):
            arrive(copies[h])
            for b in range(cb):
                at = slice(b * BLOCK, (b + 1) * BLOCK)
                own = segment(h, 5, 3, r * cb + b)
                for o in range(nr - 1):
                    own = own + landb[it, h, o, b].astype(f32)
                image[span(h), at] = own + prior_ref[:, at] * now[span(h), at]
            residual = residual - left_t(alpha[span(h)], image[span(h), :])
        if last:
            res_ref[...] = residual
        else:
            put_panel(it + 1, residual)
            gather = gather_rows(it + 1)
            resid[...] = residual
            gcb[it, c] = fold(pair_gram(residual, residual))
            gram_cols = share("col", c, nc, gcb.at[it], gcb_s.at[it], gcb_r.at[it])
            update = left_t(alpha, now[...])
            sol_ref[...] = update if it == 0 else sol_ref[...] + update
    for copy in pending:
        copy.wait_send()


def store(sol, res, sol_hbm, res_hbm, sem):
    copies = [
        pltpu.make_async_copy(src, dst, sem.at[i])
        for i, (src, dst) in enumerate(((sol, sol_hbm), (res, res_hbm)))
    ]
    for copy in copies:
        copy.start()
    for copy in copies:
        copy.wait()


def in_hbm(array):
    return pltpu.with_memory_space_constraint(array, pltpu.HBM)


def shards(right_side, prior, blocks, block_row, block_col):
    frames, pix = right_side.shape
    kb = blocks.shape[0]
    cb = pix // BLOCK
    nr = lax.axis_size("row")
    nc = lax.axis_size("col")
    nrow, ncol = cb * nc, cb * nr
    hrow, nx = nrow // 2, nc // 2
    vm = pl.BlockSpec(memory_space=pltpu.VMEM)
    dma = pltpu.SemaphoreType.DMA
    tile = (frames // PARTS, BLOCK)
    pieces = (ITERS, PARTS)
    half = (frames // 2, 2 * frames)
    out = jax.ShapeDtypeStruct(right_side.shape, f32)
    made = pl.pallas_call(
        functools.partial(kernel, nr, nc, cb, kb, frames),
        out_shape=(out, out),
        in_specs=[pl.BlockSpec(memory_space=pltpu.HBM)] * 5,
        out_specs=(vm, vm),
        scratch_shapes=[
            pltpu.VMEM((1, kb), i32),
            pltpu.VMEM((1, kb), i32),
            pltpu.VMEM((8, BLOCK), i32),
            pltpu.VMEM((8, BLOCK), f32),
            pltpu.SMEM((8, BLOCK), i32),
            pltpu.SMEM((8, BLOCK), f32),
            pltpu.VMEM(right_side.shape, f32),
            pltpu.VMEM((1, pix), f32),
            pltpu.VMEM(blocks.shape, bf16),
            pltpu.VMEM(blocks.shape, bf16),
            [pltpu.VMEM((ITERS, ncol) + tile, bf16)] * PARTS,
            [pltpu.VMEM((ITERS, nrow) + tile, bf16)] * PARTS,
            pltpu.VMEM(pieces + (hrow,) + tile, f32),
            pltpu.VMEM(pieces + (hrow,) + tile, f32),
            pltpu.VMEM(pieces + (hrow,) + tile, bf16),
            pltpu.VMEM(pieces + (nx - 1, hrow) + tile, bf16),
            pltpu.VMEM((PARTS, hrow) + tile, f32),
            pltpu.VMEM(pieces + (ncol,) + tile, bf16),
            pltpu.VMEM(pieces + (nr - 1, cb) + tile, bf16),
            pltpu.VMEM((PARTS, kb) + tile, f32),
            pltpu.VMEM(right_side.shape, f32),
            pltpu.VMEM(right_side.shape, f32),
            pltpu.VMEM(right_side.shape, f32),
            pltpu.VMEM((frames, hrow * BLOCK), f32),
            pltpu.VMEM((frames, hrow * BLOCK), f32),
            pltpu.VMEM((nc, frames, 2 * frames), f32),
            pltpu.VMEM((nr,) + half, f32),
            pltpu.VMEM((ITERS - 1, nc) + half, f32),
            pltpu.VMEM((ITERS - 1, nr) + half, f32),
            pltpu.VMEM((ITERS - 1, nc) + half, f32),
            pltpu.VMEM((ITERS, nr) + half, f32),
            dma((5,)),
            dma((2,)),
            dma(pieces + (nr - 1,)), dma(pieces + (nr - 1,)),
            dma(pieces), dma(pieces),
            dma(pieces + (nx - 1,)), dma(pieces + (nx - 1,)),
            dma(pieces), dma(pieces),
            dma(pieces + (nr - 1,)), dma(pieces + (nr - 1,)),
            dma((nc - 1,)), dma((nc - 1,)),
            dma((nr - 1,)), dma((nr - 1,)),
            dma((ITERS - 1, nc - 1)), dma((ITERS - 1, nc - 1)),
            dma((ITERS - 1, nr - 1)), dma((ITERS - 1, nr - 1)),
            dma((ITERS - 1, nc - 1)), dma((ITERS - 1, nc - 1)),
            dma((ITERS, nr - 1)), dma((ITERS, nr - 1)),
        ],
        compiler_params=pltpu.CompilerParams(
            collective_id=0, has_side_effects=True, vmem_limit_bytes=32 << 20
        ),
    )(*map(in_hbm, (block_row[None, :], block_col[None, :], right_side, prior[None, :], blocks)))
    return pl.pallas_call(
        store,
        out_shape=(out, out),
        in_specs=[pl.BlockSpec(memory_space=pl.ANY)] * 2,
        out_specs=(pl.BlockSpec(memory_space=pltpu.HBM),) * 2,
        scratch_shapes=[dma((2,))],
        compiler_params=pltpu.CompilerParams(vmem_limit_bytes=1 << 20),
    )(*made)


def solution(mesh):
    return jax.shard_map(
        shards,
        mesh=mesh,
        in_specs=(
            P("groups", ("row", "col")),
            P(("row", "col")),
            P(("row", "col"), None, None),
            P(("row", "col")),
            P(("row", "col")),
        ),
        out_specs=(P("groups", ("row", "col")), P("groups", ("row", "col"))),
        check_vma=False,
    )
```

```python
import functools

import jax
import jax.numpy as jnp
from jax import lax
from jax.experimental import pallas as pl
from jax.experimental.pallas import tpu as pltpu
from jax.sharding import PartitionSpec as P

BLOCK = 128
ITERS = 2
PARTS = 2
PIVOTS = 8
MESH = pl.DeviceIdType.MESH
HIGHEST = lax.Precision.HIGHEST
f32 = jnp.float32
bf16 = jnp.bfloat16
i32 = jnp.int32


def dot(left, right, dims):
    return lax.dot_general(
        left, right, (dims, ((), ())), precision=HIGHEST, preferred_element_type=f32
    )


def pair_gram(left, right):
    return dot(left, right, ((1,), (1,)))


def left_t(coeffs, panel):
    return dot(coeffs, panel, ((0,), (0,)))


def gauss_jordan(right, matrix, frames):
    aug = jnp.concatenate([right, matrix], axis=1)
    tiles = [aug[i : i + 8] for i in range(0, frames, 8)]
    sub = lax.broadcasted_iota(i32, tiles[0].shape, 0)
    for j in range(0, frames, PIVOTS):
        at, home, first = frames + j, j // 8, j % 8
        cols = [
            [jnp.broadcast_to(t[:, at + p : at + p + 1], t.shape) for t in tiles]
            for p in range(PIVOTS)
        ]
        lead = [tiles[home][first + q : first + q + 1] for q in range(PIVOTS)]
        small = [
            [cols[p][home][first + q : first + q + 1] for p in range(PIVOTS)]
            for q in range(PIVOTS)
        ]
        for p in range(PIVOTS):
            inverse = 1.0 / small[p][p]
            lead[p] = lead[p] * inverse
            for z in range(p + 1, PIVOTS):
                small[p][z] = small[p][z] * inverse
            for q in range(PIVOTS):
                if q != p:
                    factor = small[q][p]
                    lead[q] = lead[q] - factor * lead[p]
                    for z in range(p + 1, PIVOTS):
                        small[q][z] = small[q][z] - factor * small[p][z]
        for i in range(len(tiles)):
            new = tiles[i]
            for p in range(PIVOTS):
                new = new - cols[p][i] * lead[p]
            if i == home:
                for q in range(PIVOTS):
                    new = jnp.where(sub == first + q, lead[q], new)
            tiles[i] = new
    return jnp.concatenate(tiles, axis=0)[:, :frames]


def flip(value, mask):
    out, bit = value, 1
    while bit <= mask:
        if mask & bit:
            out = out + bit - 2 * bit * lax.rem(lax.div(value, bit), 2)
        bit *= 2
    return out


def order_by(key_row, key, other, kb):
    ids_row = lax.broadcasted_iota(i32, (1, kb), 1)
    ids = lax.broadcasted_iota(i32, (kb, 1), 0)
    lane = lax.broadcasted_iota(i32, (kb, BLOCK), 1)
    take = lambda mask, value: jnp.sum(jnp.where(mask, value, 0), axis=0, keepdims=True)
    along = lambda mask, value: jnp.sum(jnp.where(mask, value, 0), axis=1, keepdims=True)
    rank = along(key_row * kb + ids_row < key * kb + ids, 1)
    count = take(key == lane, 1)
    place = rank - along(lane < key, count)
    slot = lax.rem(place, 2)
    at = along(lane < key, lax.div(count + 1, 2)) + lax.div(place, 2)
    hots = [(at == lane) & (slot == g) for g in range(2)]
    firsts = slot == 0
    previous = take((at + 1 == lane) & firsts, key)
    keep = jnp.where((take(hots[0], key) == previous) & (lane[:1] > 0), 1, 0)
    ends = jnp.maximum(take((key <= lane) & firsts, 1) - 1, 0)
    return (
        [take(hot, ids - kb) + kb for hot in hots] + [take(hot, other) for hot in hots] + [ends],
        [keep, jnp.minimum(count, 1)],
    )


def kernel(
    nr, nc, cb, kb, frames,
    rowi_hbm, coli_hbm, rhs_hbm, prior_hbm, blocks_hbm, sol_ref, res_ref,
    rowi, coli, tabv, keepv, tab, keep, rhs_ref, prior_ref,
    blocks, turned, panels, feet, csend, cland, xsend, xland, pair, sendb, landb, scan,
    image, direct, resid, foot, adjust,
    gca, gra, gcb, grb, gcc, grk,
    in_sem, tab_sem, ag_s, ag_r, ch_s, ch_r, xh_s, xh_r, fg_s, fg_r, br_s, br_r,
    ga_s, ga_r, gb_s, gb_r, gcb_s, gcb_r, grb_s, grb_r, gcc_s, gcc_r, gk_s, gk_r,
):
    r = lax.axis_index("row")
    c = lax.axis_index("col")
    nrow, ncol = cb * nc, cb * nr
    nx = nc // 2
    hrow = nrow // 2
    half = frames // 2
    part = frames // PARTS
    side = lax.rem(lax.rem(c, 2) + lax.div(c, 2), 2)
    span = lambda h: slice(h * part, (h + 1) * part)
    pending = []

    pairs = (
        (rhs_hbm, rhs_ref), (rowi_hbm, rowi), (coli_hbm, coli), (prior_hbm, prior_ref),
        (blocks_hbm, blocks.at[pl.ds(0, kb)]),
    )
    loads = [
        pltpu.make_async_copy(src, dst, in_sem.at[i]) for i, (src, dst) in enumerate(pairs)
    ]
    for load in loads:
        load.start()

    blocks[kb] = jnp.zeros((BLOCK, BLOCK), bf16)

    barrier = pltpu.get_barrier_semaphore()
    for axis, me, n in (("row", r, nr), ("col", c, nc)):
        for m in range(n - 1, 0, -1):
            pl.semaphore_signal(
                barrier, inc=1, device_id={axis: flip(me, m)}, device_id_type=MESH
            )

    def push(axis, peer, src, dst, ssem, rsem):
        copy = pltpu.make_async_remote_copy(
            src_ref=src, dst_ref=dst, send_sem=ssem, recv_sem=rsem,
            device_id={axis: peer}, device_id_type=MESH,
        )
        copy.start()
        pending.append(copy)
        return copy

    def share(axis, me, n, buf, ssem, rsem, width=1):
        at = buf.at[pl.ds(me * width, width)]
        return [
            push(axis, flip(me, m), at, at, ssem.at[m - 1], rsem.at[m - 1])
            for m in range(n - 1, 0, -1)
        ]

    def arrive(copies):
        for copy in copies:
            copy.wait_recv()

    def total(buf, n):
        out = buf[0]
        for i in range(1, n):
            out = out + buf[i]
        return out

    def fold(gram):
        return jnp.concatenate([gram[:half], gram[half:]], axis=1)

    def unfold(packed):
        return jnp.concatenate([packed[:, :frames], packed[:, frames:]], axis=0)

    def put_panel(it, value):
        for h in range(PARTS):
            for b in range(cb):
                piece = value[span(h), b * BLOCK : (b + 1) * BLOCK]
                panels[h][it, r * cb + b] = piece.astype(bf16)

    def gather_rows(it):
        return [
            share("row", r, nr, panels[h].at[it], ag_s.at[it, h], ag_r.at[it, h], cb)
            for h in range(PARTS)
        ]

    def sweep(source, it, h, weight, count, pick, flags):
        run = jnp.zeros((part, BLOCK), f32)
        for t in range(count):
            both = [source[it, tab[pick + g, t]] for g in range(2)]
            run = run * keep[flags, t] + lax.dot_general(
                jnp.concatenate(both, axis=1), weight(t), (((1,), (0,)), ((), ())),
                preferred_element_type=f32,
            )
            scan[h, t] = run

    def forward(it, h):
        sweep(panels[h], it, h, lambda t: turned[t], (kb + nrow) // 2, 2, 0)

    def backward(it, h):
        weight = lambda t: jnp.concatenate([blocks[tab[5 + g, t]] for g in range(2)], axis=0)
        sweep(feet[h], it, h, weight, (kb + ncol) // 2, 7, 2)

    def half_square(it, which):
        wide = jnp.concatenate(
            [
                jnp.concatenate(
                    [feet[p][it, which * hrow + j] for p in range(PARTS)], axis=0
                )
                for j in range(hrow)
            ],
            axis=1,
        )
        return lax.dot_general(
            wide, wide, (((1,), (1,)), ((), ())), preferred_element_type=f32
        )

    def segment(h, end_at, valid_at, i):
        return scan[h, tab[end_at, i]] * keep[valid_at, i]

    loads[0].wait()
    put_panel(0, rhs_ref[...])
    pl.semaphore_wait(barrier, nr + nc - 2)
    gather = gather_rows(0)
    loads[1].wait()
    loads[2].wait()
    eye = lax.broadcasted_iota(i32, (kb, kb), 0) == lax.broadcasted_iota(i32, (kb, kb), 1)
    stand = lambda row: jnp.sum(jnp.where(eye, row, 0), axis=1, keepdims=True)
    bi, bj = rowi[...], coli[...]
    row_key = lax.rem(bi, nrow)
    col_key = lax.div(bj, nrow) * cb + lax.rem(bj, cb)
    row_up, col_up = stand(row_key), stand(col_key)
    ints_r, flags_r = order_by(row_key, row_up, col_up, kb)
    ints_c, flags_c = order_by(col_key, col_up, row_up, kb)
    blank = [jnp.zeros((1, BLOCK), i32)]
    tabv[...] = jnp.concatenate(ints_r + ints_c + blank * 6, axis=0)
    keepv[...] = jnp.concatenate(flags_r + flags_c + blank * 4, axis=0).astype(f32)
    tables = [
        pltpu.make_async_copy(tabv, tab, tab_sem.at[0]),
        pltpu.make_async_copy(keepv, keep, tab_sem.at[1]),
    ]
    for copy in tables:
        copy.start()
    loads[3].wait()
    rhs = rhs_ref[...]
    gca[c, :, :frames] = pair_gram(rhs, rhs)
    gca[c, :, frames:] = pair_gram(rhs, prior_ref[...] * rhs)
    gram_cols = share("col", c, nc, gca, ga_s, ga_r)
    for copy in tables:
        copy.wait()
    loads[4].wait()

    def turn(t, _):
        for g in range(2):
            turned[t, g * BLOCK : (g + 1) * BLOCK] = blocks[tab[g, t]].T
        return 0

    lax.fori_loop(0, (kb + nrow) // 2, turn, 0, unroll=8)
    arrive(gram_cols)
    sums = total(gca, nc)
    gra[r] = fold(sums[:, :frames])
    weighted = fold(sums[:, frames:])
    gram_rows = share("row", r, nr, gra, gb_s, gb_r)
    gram = inverse = alpha = None

    for it in range(ITERS):
        last = it + 1 == ITERS
        if it > 0:
            arrive(gram_cols)
            grb[it - 1, r] = total(gcb.at[it - 1], nc)
            gram_rows = share(
                "row", r, nr, grb.at[it - 1], grb_s.at[it - 1], grb_r.at[it - 1]
            )
        crossed = []
        for h in range(PARTS):
            arrive(gather[h])
            forward(it, h)
            for j in range(hrow):
                csend[it, h, j] = segment(h, 4, 1, (1 - side) * hrow + j)
            swapped = push(
                "col", flip(c, 1), csend.at[it, h], cland.at[it, h],
                ch_s.at[it, h], ch_r.at[it, h],
            )
            arrive([swapped])
            for j in range(hrow):
                own = segment(h, 4, 1, side * hrow + j) + cland[it, h, j]
                pair[h, j] = own
                xsend[it, h, j] = own.astype(bf16)
            crossed.append([
                push(
                    "col", flip(c, 2 * m + m % 2), xsend.at[it, h], xland.at[it, h, m - 1],
                    xh_s.at[it, h, m - 1], xh_r.at[it, h, m - 1],
                )
                for m in range(nx - 1, 0, -1)
            ])
        if it > 0:
            arrive(gram_rows)
            gram = unfold(total(grb.at[it - 1], nr))
            beta = dot(inverse, gram, ((1,), (0,)))
            adjust[...] = left_t(beta, foot[...])
        copies = []
        for h in range(PARTS):
            arrive(crossed[h])
            for j in range(hrow):
                at = slice(j * BLOCK, (j + 1) * BLOCK)
                own = pair[h, j]
                for m in range(nx - 1):
                    own = own + xland[it, h, m, j].astype(f32)
                if it > 0:
                    own = own + adjust[span(h), at]
                if not last:
                    foot[span(h), at] = own
                feet[h][it, side * hrow + j] = own.astype(bf16)
            at = feet[h].at[it, pl.ds(side * hrow, hrow)]
            spread = push("col", flip(c, 1), at, at, fg_s.at[it, h], fg_r.at[it, h])
            if it > 0 and h == 0:
                before = (rhs_ref if it == 1 else direct)[...]
                direct[...] = resid[...] + left_t(beta, before)
                direction = direct[...]
                gcc[it - 1, c] = fold(pair_gram(direction, prior_ref[...] * direction))
                weight_cols = share(
                    "col", c, nc, gcc.at[it - 1], gcc_s.at[it - 1], gcc_r.at[it - 1]
                )
            if h + 1 == PARTS:
                square = half_square(it, side)
            arrive([spread])
            if h + 1 == PARTS:
                square = square + half_square(it, 1 - side)
                if it > 0:
                    arrive(weight_cols)
                    weighted = total(gcc.at[it - 1], nc)
                grk[it, r] = fold(square) + weighted
                curve_rows = share("row", r, nr, grk.at[it], gk_s.at[it], gk_r.at[it])
            backward(it, h)
            for i in range(ncol):
                sendb[it, h, i] = segment(h, 9, 3, i).astype(bf16)
            copies.append([
                push(
                    "row", flip(r, m), sendb.at[it, h, pl.ds(flip(r, m) * cb, cb)],
                    landb.at[it, h, m - 1], br_s.at[it, h, m - 1], br_r.at[it, h, m - 1],
                )
                for m in range(nr - 1, 0, -1)
            ])
        if it == 0:
            arrive(gram_rows)
            gram = unfold(total(gra, nr))
        if not last:
            square = (frames, frames)
            ones = lax.broadcasted_iota(i32, square, 0) == lax.broadcasted_iota(i32, square, 1)
            inverse = gauss_jordan(jnp.where(ones, 1.0, 0.0), gram, frames)
        arrive(curve_rows)
        alpha = gauss_jordan(gram, unfold(total(grk.at[it], nr)), frames)
        now = rhs_ref if it == 0 else direct
        if last:
            update = left_t(alpha, now[...])
            sol_ref[...] = update if it == 0 else sol_ref[...] + update
        residual = (rhs_ref if it == 0 else resid)[...]
        for h in range(PARTS):
            arrive(copies[h])
            for b in range(cb):
                at = slice(b * BLOCK, (b + 1) * BLOCK)
                own = segment(h, 9, 3, r * cb + b)
                for o in range(nr - 1):
                    own = own + landb[it, h, o, b].astype(f32)
                image[span(h), at] = own + prior_ref[:, at] * now[span(h), at]
            residual = residual - left_t(alpha[span(h)], image[span(h), :])
        if last:
            res_ref[...] = residual
        else:
            put_panel(it + 1, residual)
            gather = gather_rows(it + 1)
            resid[...] = residual
            gcb[it, c] = fold(pair_gram(residual, residual))
            gram_cols = share("col", c, nc, gcb.at[it], gcb_s.at[it], gcb_r.at[it])
            update = left_t(alpha, now[...])
            sol_ref[...] = update if it == 0 else sol_ref[...] + update
    for copy in pending:
        copy.wait_send()


def store(sol, res, sol_hbm, res_hbm, sem):
    copies = [
        pltpu.make_async_copy(src, dst, sem.at[i])
        for i, (src, dst) in enumerate(((sol, sol_hbm), (res, res_hbm)))
    ]
    for copy in copies:
        copy.start()
    for copy in copies:
        copy.wait()


def in_hbm(array):
    return pltpu.with_memory_space_constraint(array, pltpu.HBM)


def shards(right_side, prior, blocks, block_row, block_col):
    frames, pix = right_side.shape
    kb = blocks.shape[0]
    cb = pix // BLOCK
    nr = lax.axis_size("row")
    nc = lax.axis_size("col")
    nrow, ncol = cb * nc, cb * nr
    hrow, nx = nrow // 2, nc // 2
    vm = pl.BlockSpec(memory_space=pltpu.VMEM)
    dma = pltpu.SemaphoreType.DMA
    tile = (frames // PARTS, BLOCK)
    pieces = (ITERS, PARTS)
    half = (frames // 2, 2 * frames)
    out = jax.ShapeDtypeStruct(right_side.shape, f32)
    made = pl.pallas_call(
        functools.partial(kernel, nr, nc, cb, kb, frames),
        out_shape=(out, out),
        in_specs=[pl.BlockSpec(memory_space=pltpu.HBM)] * 5,
        out_specs=(vm, vm),
        scratch_shapes=[
            pltpu.VMEM((1, kb), i32),
            pltpu.VMEM((1, kb), i32),
            pltpu.VMEM((16, BLOCK), i32),
            pltpu.VMEM((8, BLOCK), f32),
            pltpu.SMEM((16, BLOCK), i32),
            pltpu.SMEM((8, BLOCK), f32),
            pltpu.VMEM(right_side.shape, f32),
            pltpu.VMEM((1, pix), f32),
            pltpu.VMEM((kb + 1, BLOCK, BLOCK), bf16),
            pltpu.VMEM(((kb + nrow) // 2, 2 * BLOCK, BLOCK), bf16),
            [pltpu.VMEM((ITERS, ncol) + tile, bf16)] * PARTS,
            [pltpu.VMEM((ITERS, nrow) + tile, bf16)] * PARTS,
            pltpu.VMEM(pieces + (hrow,) + tile, f32),
            pltpu.VMEM(pieces + (hrow,) + tile, f32),
            pltpu.VMEM(pieces + (hrow,) + tile, bf16),
            pltpu.VMEM(pieces + (nx - 1, hrow) + tile, bf16),
            pltpu.VMEM((PARTS, hrow) + tile, f32),
            pltpu.VMEM(pieces + (ncol,) + tile, bf16),
            pltpu.VMEM(pieces + (nr - 1, cb) + tile, bf16),
            pltpu.VMEM((PARTS, (kb + max(nrow, ncol)) // 2) + tile, f32),
            pltpu.VMEM(right_side.shape, f32),
            pltpu.VMEM(right_side.shape, f32),
            pltpu.VMEM(right_side.shape, f32),
            pltpu.VMEM((frames, hrow * BLOCK), f32),
            pltpu.VMEM((frames, hrow * BLOCK), f32),
            pltpu.VMEM((nc, frames, 2 * frames), f32),
            pltpu.VMEM((nr,) + half, f32),
            pltpu.VMEM((ITERS - 1, nc) + half, f32),
            pltpu.VMEM((ITERS - 1, nr) + half, f32),
            pltpu.VMEM((ITERS - 1, nc) + half, f32),
            pltpu.VMEM((ITERS, nr) + half, f32),
            dma((5,)),
            dma((2,)),
            dma(pieces + (nr - 1,)), dma(pieces + (nr - 1,)),
            dma(pieces), dma(pieces),
            dma(pieces + (nx - 1,)), dma(pieces + (nx - 1,)),
            dma(pieces), dma(pieces),
            dma(pieces + (nr - 1,)), dma(pieces + (nr - 1,)),
            dma((nc - 1,)), dma((nc - 1,)),
            dma((nr - 1,)), dma((nr - 1,)),
            dma((ITERS - 1, nc - 1)), dma((ITERS - 1, nc - 1)),
            dma((ITERS - 1, nr - 1)), dma((ITERS - 1, nr - 1)),
            dma((ITERS - 1, nc - 1)), dma((ITERS - 1, nc - 1)),
            dma((ITERS, nr - 1)), dma((ITERS, nr - 1)),
        ],
        compiler_params=pltpu.CompilerParams(
            collective_id=0, has_side_effects=True, vmem_limit_bytes=32 << 20
        ),
    )(*map(in_hbm, (block_row[None, :], block_col[None, :], right_side, prior[None, :], blocks)))
    return pl.pallas_call(
        store,
        out_shape=(out, out),
        in_specs=[pl.BlockSpec(memory_space=pl.ANY)] * 2,
        out_specs=(pl.BlockSpec(memory_space=pltpu.HBM),) * 2,
        scratch_shapes=[dma((2,))],
        compiler_params=pltpu.CompilerParams(vmem_limit_bytes=1 << 20),
    )(*made)


def solution(mesh):
    return jax.shard_map(
        shards,
        mesh=mesh,
        in_specs=(
            P("groups", ("row", "col")),
            P(("row", "col")),
            P(("row", "col"), None, None),
            P(("row", "col")),
            P(("row", "col")),
        ),
        out_specs=(P("groups", ("row", "col")), P("groups", ("row", "col"))),
        check_vma=False,
    )
```

```python
import functools

import jax
import jax.numpy as jnp
from jax import lax
from jax.experimental import pallas as pl
from jax.experimental.pallas import tpu as pltpu
from jax.sharding import PartitionSpec as P

BLOCK = 128
ITERS = 2
PARTS = 2
PIVOTS = 16
MESH = pl.DeviceIdType.MESH
HIGHEST = lax.Precision.HIGHEST
f32 = jnp.float32
bf16 = jnp.bfloat16
i32 = jnp.int32


def dot(left, right, dims):
    return lax.dot_general(
        left, right, (dims, ((), ())), precision=HIGHEST, preferred_element_type=f32
    )


def pair_gram(left, right):
    return dot(left, right, ((1,), (1,)))


def left_t(coeffs, panel):
    return dot(coeffs, panel, ((0,), (0,)))


def gauss_jordan(right, matrix, frames):
    aug = jnp.concatenate([right, matrix], axis=1)
    tiles = [aug[i : i + 8] for i in range(0, frames, 8)]
    sub = lax.broadcasted_iota(i32, tiles[0].shape, 0)
    spread = lambda tile, row: jnp.broadcast_to(tile[row : row + 1], tile.shape)
    deep = PIVOTS // 8
    for j in range(0, frames, PIVOTS):
        at, home = frames + j, j // 8
        cols = [
            [jnp.broadcast_to(t[:, at + p : at + p + 1], t.shape) for t in tiles]
            for p in range(PIVOTS)
        ]
        strip = tiles[home : home + deep]
        small = [cols[p][home : home + deep] for p in range(PIVOTS)]
        for p in range(PIVOTS):
            own, row = p // 8, p % 8
            inverse = 1.0 / spread(small[p][own], row)
            lead = spread(strip[own], row) * inverse
            leads = {z: spread(small[z][own], row) * inverse for z in range(p + 1, PIVOTS)}
            for i in range(deep):
                factor = small[p][i]
                put = lambda old, new: (
                    jnp.where(sub == row, new, old - factor * new)
                    if i == own
                    else old - factor * new
                )
                strip[i] = put(strip[i], lead)
                for z, value in leads.items():
                    small[z][i] = put(small[z][i], value)
        for i in range(frames // 8):
            if home <= i < home + deep:
                tiles[i] = strip[i - home]
                continue
            for p in range(PIVOTS):
                tiles[i] = tiles[i] - cols[p][i] * spread(strip[p // 8], p % 8)
    return jnp.concatenate(tiles, axis=0)[:, :frames]


def flip(value, mask):
    out, bit = value, 1
    while bit <= mask:
        if mask & bit:
            out = out + bit - 2 * bit * lax.rem(lax.div(value, bit), 2)
        bit *= 2
    return out


def order_by(key_row, key, other, kb):
    ids_row = lax.broadcasted_iota(i32, (1, kb), 1)
    ids = lax.broadcasted_iota(i32, (kb, 1), 0)
    lane = lax.broadcasted_iota(i32, (kb, BLOCK), 1)
    take = lambda mask, value: jnp.sum(jnp.where(mask, value, 0), axis=0, keepdims=True)
    along = lambda mask, value: jnp.sum(jnp.where(mask, value, 0), axis=1, keepdims=True)
    rank = along(key_row * kb + ids_row < key * kb + ids, 1)
    count = take(key == lane, 1)
    place = rank - along(lane < key, count)
    slot = lax.rem(place, 2)
    at = along(lane < key, lax.div(count + 1, 2)) + lax.div(place, 2)
    hots = [(at == lane) & (slot == g) for g in range(2)]
    firsts = slot == 0
    previous = take((at + 1 == lane) & firsts, key)
    keep = jnp.where((take(hots[0], key) == previous) & (lane[:1] > 0), 1, 0)
    ends = jnp.maximum(take((key <= lane) & firsts, 1) - 1, 0)
    return (
        [take(hot, ids - kb) + kb for hot in hots] + [take(hot, other) for hot in hots] + [ends],
        [keep, jnp.minimum(count, 1)],
    )


def kernel(
    nr, nc, cb, kb, frames,
    rowi_hbm, coli_hbm, rhs_hbm, prior_hbm, blocks_hbm, sol_ref, res_ref,
    rowi, coli, tabv, keepv, tab, keep, rhs_ref, prior_ref,
    blocks, turned, panels, feet, csend, cland, xsend, xland, pair, sendb, landb, scan,
    image, direct, resid, foot, adjust,
    gca, gra, gcb, grb, gcc, grk,
    in_sem, tab_sem, ag_s, ag_r, ch_s, ch_r, xh_s, xh_r, fg_s, fg_r, br_s, br_r,
    ga_s, ga_r, gb_s, gb_r, gcb_s, gcb_r, grb_s, grb_r, gcc_s, gcc_r, gk_s, gk_r,
):
    r = lax.axis_index("row")
    c = lax.axis_index("col")
    nrow, ncol = cb * nc, cb * nr
    nx = nc // 2
    hrow = nrow // 2
    half = frames // 2
    part = frames // PARTS
    side = lax.rem(lax.rem(c, 2) + lax.div(c, 2), 2)
    span = lambda h: slice(h * part, (h + 1) * part)
    pending = []

    pairs = (
        (rhs_hbm, rhs_ref), (rowi_hbm, rowi), (coli_hbm, coli), (prior_hbm, prior_ref),
        (blocks_hbm, blocks.at[pl.ds(0, kb)]),
    )
    loads = [
        pltpu.make_async_copy(src, dst, in_sem.at[i]) for i, (src, dst) in enumerate(pairs)
    ]
    for load in loads:
        load.start()

    blocks[kb] = jnp.zeros((BLOCK, BLOCK), bf16)

    barrier = pltpu.get_barrier_semaphore()
    for axis, me, n in (("row", r, nr), ("col", c, nc)):
        for m in range(n - 1, 0, -1):
            pl.semaphore_signal(
                barrier, inc=1, device_id={axis: flip(me, m)}, device_id_type=MESH
            )

    def push(axis, peer, src, dst, ssem, rsem):
        copy = pltpu.make_async_remote_copy(
            src_ref=src, dst_ref=dst, send_sem=ssem, recv_sem=rsem,
            device_id={axis: peer}, device_id_type=MESH,
        )
        copy.start()
        pending.append(copy)
        return copy

    def share(axis, me, n, buf, ssem, rsem, width=1):
        at = buf.at[pl.ds(me * width, width)]
        return [
            push(axis, flip(me, m), at, at, ssem.at[m - 1], rsem.at[m - 1])
            for m in range(n - 1, 0, -1)
        ]

    def arrive(copies):
        for copy in copies:
            copy.wait_recv()

    def total(buf, n):
        out = buf[0]
        for i in range(1, n):
            out = out + buf[i]
        return out

    def fold(gram):
        return jnp.concatenate([gram[:half], gram[half:]], axis=1)

    def unfold(packed):
        return jnp.concatenate([packed[:, :frames], packed[:, frames:]], axis=0)

    def put_panel(it, value):
        for h in range(PARTS):
            for b in range(cb):
                piece = value[span(h), b * BLOCK : (b + 1) * BLOCK]
                panels[h][it, r * cb + b] = piece.astype(bf16)

    def gather_rows(it):
        return [
            share("row", r, nr, panels[h].at[it], ag_s.at[it, h], ag_r.at[it, h], cb)
            for h in range(PARTS)
        ]

    def sweep(source, it, h, weight, count, pick, flags):
        run = jnp.zeros((part, BLOCK), f32)
        for t in range(count):
            both = [source[it, tab[pick + g, t]] for g in range(2)]
            run = run * keep[flags, t] + lax.dot_general(
                jnp.concatenate(both, axis=1), weight(t), (((1,), (0,)), ((), ())),
                preferred_element_type=f32,
            )
            scan[h, t] = run

    def forward(it, h):
        sweep(panels[h], it, h, lambda t: turned[t], (kb + nrow) // 2, 2, 0)

    def backward(it, h):
        weight = lambda t: jnp.concatenate([blocks[tab[5 + g, t]] for g in range(2)], axis=0)
        sweep(feet[h], it, h, weight, (kb + ncol) // 2, 7, 2)

    def half_square(it, which):
        wide = jnp.concatenate(
            [
                jnp.concatenate(
                    [feet[p][it, which * hrow + j] for p in range(PARTS)], axis=0
                )
                for j in range(hrow)
            ],
            axis=1,
        )
        return lax.dot_general(
            wide, wide, (((1,), (1,)), ((), ())), preferred_element_type=f32
        )

    def segment(h, end_at, valid_at, i):
        return scan[h, tab[end_at, i]] * keep[valid_at, i]

    loads[0].wait()
    put_panel(0, rhs_ref[...])
    pl.semaphore_wait(barrier, nr + nc - 2)
    gather = gather_rows(0)
    loads[1].wait()
    loads[2].wait()
    eye = lax.broadcasted_iota(i32, (kb, kb), 0) == lax.broadcasted_iota(i32, (kb, kb), 1)
    stand = lambda row: jnp.sum(jnp.where(eye, row, 0), axis=1, keepdims=True)
    bi, bj = rowi[...], coli[...]
    row_key = lax.rem(bi, nrow)
    col_key = lax.div(bj, nrow) * cb + lax.rem(bj, cb)
    row_up, col_up = stand(row_key), stand(col_key)
    ints_r, flags_r = order_by(row_key, row_up, col_up, kb)
    ints_c, flags_c = order_by(col_key, col_up, row_up, kb)
    blank = [jnp.zeros((1, BLOCK), i32)]
    tabv[...] = jnp.concatenate(ints_r + ints_c + blank * 6, axis=0)
    keepv[...] = jnp.concatenate(flags_r + flags_c + blank * 4, axis=0).astype(f32)
    tables = [
        pltpu.make_async_copy(tabv, tab, tab_sem.at[0]),
        pltpu.make_async_copy(keepv, keep, tab_sem.at[1]),
    ]
    for copy in tables:
        copy.start()
    loads[3].wait()
    rhs = rhs_ref[...]
    gca[c, :, :frames] = pair_gram(rhs, rhs)
    gca[c, :, frames:] = pair_gram(rhs, prior_ref[...] * rhs)
    gram_cols = share("col", c, nc, gca, ga_s, ga_r)
    for copy in tables:
        copy.wait()
    loads[4].wait()

    def turn(t, _):
        for g in range(2):
            turned[t, g * BLOCK : (g + 1) * BLOCK] = blocks[tab[g, t]].T
        return 0

    lax.fori_loop(0, (kb + nrow) // 2, turn, 0, unroll=8)
    arrive(gram_cols)
    sums = total(gca, nc)
    gra[r] = fold(sums[:, :frames])
    weighted = fold(sums[:, frames:])
    gram_rows = share("row", r, nr, gra, gb_s, gb_r)
    gram = inverse = alpha = None

    for it in range(ITERS):
        last = it + 1 == ITERS
        if it > 0:
            arrive(gram_cols)
            grb[it - 1, r] = total(gcb.at[it - 1], nc)
            gram_rows = share(
                "row", r, nr, grb.at[it - 1], grb_s.at[it - 1], grb_r.at[it - 1]
            )
        crossed = []
        for h in range(PARTS):
            arrive(gather[h])
            forward(it, h)
            for j in range(hrow):
                csend[it, h, j] = segment(h, 4, 1, (1 - side) * hrow + j)
            swapped = push(
                "col", flip(c, 1), csend.at[it, h], cland.at[it, h],
                ch_s.at[it, h], ch_r.at[it, h],
            )
            arrive([swapped])
            for j in range(hrow):
                own = segment(h, 4, 1, side * hrow + j) + cland[it, h, j]
                pair[h, j] = own
                xsend[it, h, j] = own.astype(bf16)
            crossed.append([
                push(
                    "col", flip(c, 2 * m + m % 2), xsend.at[it, h], xland.at[it, h, m - 1],
                    xh_s.at[it, h, m - 1], xh_r.at[it, h, m - 1],
                )
                for m in range(nx - 1, 0, -1)
            ])
        if it > 0:
            arrive(gram_rows)
            gram = unfold(total(grb.at[it - 1], nr))
            beta = dot(inverse, gram, ((1,), (0,)))
            adjust[...] = left_t(beta, foot[...])
        copies = []
        for h in range(PARTS):
            arrive(crossed[h])
            for j in range(hrow):
                at = slice(j * BLOCK, (j + 1) * BLOCK)
                own = pair[h, j]
                for m in range(nx - 1):
                    own = own + xland[it, h, m, j].astype(f32)
                if it > 0:
                    own = own + adjust[span(h), at]
                if not last:
                    foot[span(h), at] = own
                feet[h][it, side * hrow + j] = own.astype(bf16)
            at = feet[h].at[it, pl.ds(side * hrow, hrow)]
            spread = push("col", flip(c, 1), at, at, fg_s.at[it, h], fg_r.at[it, h])
            if it > 0 and h == 0:
                before = (rhs_ref if it == 1 else direct)[...]
                direct[...] = resid[...] + left_t(beta, before)
                direction = direct[...]
                gcc[it - 1, c] = fold(pair_gram(direction, prior_ref[...] * direction))
                weight_cols = share(
                    "col", c, nc, gcc.at[it - 1], gcc_s.at[it - 1], gcc_r.at[it - 1]
                )
            if h + 1 == PARTS:
                square = half_square(it, side)
            arrive([spread])
            if h + 1 == PARTS:
                square = square + half_square(it, 1 - side)
                if it > 0:
                    arrive(weight_cols)
                    weighted = total(gcc.at[it - 1], nc)
                grk[it, r] = fold(square) + weighted
                curve_rows = share("row", r, nr, grk.at[it], gk_s.at[it], gk_r.at[it])
            backward(it, h)
            for i in range(ncol):
                sendb[it, h, i] = segment(h, 9, 3, i).astype(bf16)
            copies.append([
                push(
                    "row", flip(r, m), sendb.at[it, h, pl.ds(flip(r, m) * cb, cb)],
                    landb.at[it, h, m - 1], br_s.at[it, h, m - 1], br_r.at[it, h, m - 1],
                )
                for m in range(nr - 1, 0, -1)
            ])
        if it == 0:
            arrive(gram_rows)
            gram = unfold(total(gra, nr))
        if not last:
            square = (frames, frames)
            ones = lax.broadcasted_iota(i32, square, 0) == lax.broadcasted_iota(i32, square, 1)
            inverse = gauss_jordan(jnp.where(ones, 1.0, 0.0), gram, frames)
        now = rhs_ref if it == 0 else direct
        for h in range(PARTS):
            if h + 1 == PARTS:
                arrive(curve_rows)
                alpha = gauss_jordan(gram, unfold(total(grk.at[it], nr)), frames)
                if last:
                    update = left_t(alpha, now[...])
                    sol_ref[...] = update if it == 0 else sol_ref[...] + update
            arrive(copies[h])
            for b in range(cb):
                at = slice(b * BLOCK, (b + 1) * BLOCK)
                own = segment(h, 9, 3, r * cb + b)
                for o in range(nr - 1):
                    own = own + landb[it, h, o, b].astype(f32)
                image[span(h), at] = own + prior_ref[:, at] * now[span(h), at]
        residual = (rhs_ref if it == 0 else resid)[...] - left_t(alpha, image[...])
        if last:
            res_ref[...] = residual
        else:
            put_panel(it + 1, residual)
            gather = gather_rows(it + 1)
            resid[...] = residual
            gcb[it, c] = fold(pair_gram(residual, residual))
            gram_cols = share("col", c, nc, gcb.at[it], gcb_s.at[it], gcb_r.at[it])
            update = left_t(alpha, now[...])
            sol_ref[...] = update if it == 0 else sol_ref[...] + update
    for copy in pending:
        copy.wait_send()


def store(sol, res, sol_hbm, res_hbm, sem):
    copies = [
        pltpu.make_async_copy(src, dst, sem.at[i])
        for i, (src, dst) in enumerate(((sol, sol_hbm), (res, res_hbm)))
    ]
    for copy in copies:
        copy.start()
    for copy in copies:
        copy.wait()


def in_hbm(array):
    return pltpu.with_memory_space_constraint(array, pltpu.HBM)


def shards(right_side, prior, blocks, block_row, block_col):
    frames, pix = right_side.shape
    kb = blocks.shape[0]
    cb = pix // BLOCK
    nr = lax.axis_size("row")
    nc = lax.axis_size("col")
    nrow, ncol = cb * nc, cb * nr
    hrow, nx = nrow // 2, nc // 2
    vm = pl.BlockSpec(memory_space=pltpu.VMEM)
    dma = pltpu.SemaphoreType.DMA
    tile = (frames // PARTS, BLOCK)
    pieces = (ITERS, PARTS)
    half = (frames // 2, 2 * frames)
    out = jax.ShapeDtypeStruct(right_side.shape, f32)
    made = pl.pallas_call(
        functools.partial(kernel, nr, nc, cb, kb, frames),
        out_shape=(out, out),
        in_specs=[pl.BlockSpec(memory_space=pltpu.HBM)] * 5,
        out_specs=(vm, vm),
        scratch_shapes=[
            pltpu.VMEM((1, kb), i32),
            pltpu.VMEM((1, kb), i32),
            pltpu.VMEM((16, BLOCK), i32),
            pltpu.VMEM((8, BLOCK), f32),
            pltpu.SMEM((16, BLOCK), i32),
            pltpu.SMEM((8, BLOCK), f32),
            pltpu.VMEM(right_side.shape, f32),
            pltpu.VMEM((1, pix), f32),
            pltpu.VMEM((kb + 1, BLOCK, BLOCK), bf16),
            pltpu.VMEM(((kb + nrow) // 2, 2 * BLOCK, BLOCK), bf16),
            [pltpu.VMEM((ITERS, ncol) + tile, bf16)] * PARTS,
            [pltpu.VMEM((ITERS, nrow) + tile, bf16)] * PARTS,
            pltpu.VMEM(pieces + (hrow,) + tile, f32),
            pltpu.VMEM(pieces + (hrow,) + tile, f32),
            pltpu.VMEM(pieces + (hrow,) + tile, bf16),
            pltpu.VMEM(pieces + (nx - 1, hrow) + tile, bf16),
            pltpu.VMEM((PARTS, hrow) + tile, f32),
            pltpu.VMEM(pieces + (ncol,) + tile, bf16),
            pltpu.VMEM(pieces + (nr - 1, cb) + tile, bf16),
            pltpu.VMEM((PARTS, (kb + max(nrow, ncol)) // 2) + tile, f32),
            pltpu.VMEM(right_side.shape, f32),
            pltpu.VMEM(right_side.shape, f32),
            pltpu.VMEM(right_side.shape, f32),
            pltpu.VMEM((frames, hrow * BLOCK), f32),
            pltpu.VMEM((frames, hrow * BLOCK), f32),
            pltpu.VMEM((nc, frames, 2 * frames), f32),
            pltpu.VMEM((nr,) + half, f32),
            pltpu.VMEM((ITERS - 1, nc) + half, f32),
            pltpu.VMEM((ITERS - 1, nr) + half, f32),
            pltpu.VMEM((ITERS - 1, nc) + half, f32),
            pltpu.VMEM((ITERS, nr) + half, f32),
            dma((5,)),
            dma((2,)),
            dma(pieces + (nr - 1,)), dma(pieces + (nr - 1,)),
            dma(pieces), dma(pieces),
            dma(pieces + (nx - 1,)), dma(pieces + (nx - 1,)),
            dma(pieces), dma(pieces),
            dma(pieces + (nr - 1,)), dma(pieces + (nr - 1,)),
            dma((nc - 1,)), dma((nc - 1,)),
            dma((nr - 1,)), dma((nr - 1,)),
            dma((ITERS - 1, nc - 1)), dma((ITERS - 1, nc - 1)),
            dma((ITERS - 1, nr - 1)), dma((ITERS - 1, nr - 1)),
            dma((ITERS - 1, nc - 1)), dma((ITERS - 1, nc - 1)),
            dma((ITERS, nr - 1)), dma((ITERS, nr - 1)),
        ],
        compiler_params=pltpu.CompilerParams(
            collective_id=0, has_side_effects=True, vmem_limit_bytes=32 << 20
        ),
    )(*map(in_hbm, (block_row[None, :], block_col[None, :], right_side, prior[None, :], blocks)))
    return pl.pallas_call(
        store,
        out_shape=(out, out),
        in_specs=[pl.BlockSpec(memory_space=pl.ANY)] * 2,
        out_specs=(pl.BlockSpec(memory_space=pltpu.HBM),) * 2,
        scratch_shapes=[dma((2,))],
        compiler_params=pltpu.CompilerParams(vmem_limit_bytes=1 << 20),
    )(*made)


def solution(mesh):
    return jax.shard_map(
        shards,
        mesh=mesh,
        in_specs=(
            P("groups", ("row", "col")),
            P(("row", "col")),
            P(("row", "col"), None, None),
            P(("row", "col")),
            P(("row", "col")),
        ),
        out_specs=(P("groups", ("row", "col")), P("groups", ("row", "col"))),
        check_vma=False,
    )
```

```python
import functools

import jax
import jax.numpy as jnp
from jax import lax
from jax.experimental import pallas as pl
from jax.experimental.pallas import tpu as pltpu
from jax.sharding import PartitionSpec as P

BLOCK = 128
ITERS = 2
PARTS = 2
PIVOTS = 16
MESH = pl.DeviceIdType.MESH
HIGHEST = lax.Precision.HIGHEST
f32 = jnp.float32
bf16 = jnp.bfloat16
i32 = jnp.int32


def dot(left, right, dims):
    return lax.dot_general(
        left, right, (dims, ((), ())), precision=HIGHEST, preferred_element_type=f32
    )


def pair_gram(left, right):
    return dot(left, right, ((1,), (1,)))


def left_t(coeffs, panel):
    return dot(coeffs, panel, ((0,), (0,)))


def gauss_jordan(right, matrix, frames):
    aug = jnp.concatenate([right, matrix], axis=1)
    tiles = [aug[i : i + 8] for i in range(0, frames, 8)]
    sub = lax.broadcasted_iota(i32, tiles[0].shape, 0)
    spread = lambda tile, row: jnp.broadcast_to(tile[row : row + 1], tile.shape)
    deep = PIVOTS // 8
    for j in range(0, frames, PIVOTS):
        at, home = frames + j, j // 8
        cols = [
            [jnp.broadcast_to(t[:, at + p : at + p + 1], t.shape) for t in tiles]
            for p in range(PIVOTS)
        ]
        strip = tiles[home : home + deep]
        small = [cols[p][home : home + deep] for p in range(PIVOTS)]
        for p in range(PIVOTS):
            own, row = p // 8, p % 8
            inverse = 1.0 / spread(small[p][own], row)
            lead = spread(strip[own], row) * inverse
            leads = {z: spread(small[z][own], row) * inverse for z in range(p + 1, PIVOTS)}
            for i in range(deep):
                factor = small[p][i]
                put = lambda old, new: (
                    jnp.where(sub == row, new, old - factor * new)
                    if i == own
                    else old - factor * new
                )
                strip[i] = put(strip[i], lead)
                for z, value in leads.items():
                    small[z][i] = put(small[z][i], value)
        for i in range(frames // 8):
            if home <= i < home + deep:
                tiles[i] = strip[i - home]
                continue
            for p in range(PIVOTS):
                tiles[i] = tiles[i] - cols[p][i] * spread(strip[p // 8], p % 8)
    return jnp.concatenate(tiles, axis=0)[:, :frames]


def flip(value, mask):
    out, bit = value, 1
    while bit <= mask:
        if mask & bit:
            out = out + bit - 2 * bit * lax.rem(lax.div(value, bit), 2)
        bit *= 2
    return out


def order_by(key_row, key, other, kb):
    ids_row = lax.broadcasted_iota(i32, (1, kb), 1)
    ids = lax.broadcasted_iota(i32, (kb, 1), 0)
    lane = lax.broadcasted_iota(i32, (kb, BLOCK), 1)
    take = lambda mask, value: jnp.sum(jnp.where(mask, value, 0), axis=0, keepdims=True)
    along = lambda mask, value: jnp.sum(jnp.where(mask, value, 0), axis=1, keepdims=True)
    rank = along(key_row * kb + ids_row < key * kb + ids, 1)
    count = take(key == lane, 1)
    place = rank - along(lane < key, count)
    slot = lax.rem(place, 2)
    at = along(lane < key, lax.div(count + 1, 2)) + lax.div(place, 2)
    hots = [(at == lane) & (slot == g) for g in range(2)]
    firsts = slot == 0
    previous = take((at + 1 == lane) & firsts, key)
    keep = jnp.where((take(hots[0], key) == previous) & (lane[:1] > 0), 1, 0)
    ends = jnp.maximum(take((key <= lane) & firsts, 1) - 1, 0)
    return (
        [take(hot, ids - kb) + kb for hot in hots] + [take(hot, other) for hot in hots] + [ends],
        [keep, jnp.minimum(count, 1)],
    )


def kernel(
    nr, nc, cb, kb, frames,
    rowi_hbm, coli_hbm, rhs_hbm, prior_hbm, blocks_hbm, sol_ref, res_ref,
    rowi, coli, tabv, keepv, tab, keep, rhs_ref, prior_ref,
    blocks, turned, panels, feet, csend, cland, xsend, xland, pair, sendb, landb, scan,
    image, direct, resid, foot, adjust,
    gca, gra, gcb, grb, gcc, grk,
    in_sem, tab_sem, ag_s, ag_r, ch_s, ch_r, xh_s, xh_r, fg_s, fg_r, br_s, br_r,
    ga_s, ga_r, gb_s, gb_r, gcb_s, gcb_r, grb_s, grb_r, gcc_s, gcc_r, gk_s, gk_r,
):
    r = lax.axis_index("row")
    c = lax.axis_index("col")
    nrow, ncol = cb * nc, cb * nr
    nx = nc // 2
    hrow = nrow // 2
    half = frames // 2
    part = frames // PARTS
    side = lax.rem(lax.rem(c, 2) + lax.div(c, 2), 2)
    span = lambda h: slice(h * part, (h + 1) * part)
    pending = []

    pairs = (
        (rhs_hbm, rhs_ref), (rowi_hbm, rowi), (coli_hbm, coli), (prior_hbm, prior_ref),
        (blocks_hbm, blocks.at[pl.ds(0, kb)]),
    )
    loads = [
        pltpu.make_async_copy(src, dst, in_sem.at[i]) for i, (src, dst) in enumerate(pairs)
    ]
    for load in loads:
        load.start()

    blocks[kb] = jnp.zeros((BLOCK, BLOCK), bf16)

    barrier = pltpu.get_barrier_semaphore()
    for axis, me, n in (("row", r, nr), ("col", c, nc)):
        for m in range(n - 1, 0, -1):
            pl.semaphore_signal(
                barrier, inc=1, device_id={axis: flip(me, m)}, device_id_type=MESH
            )

    def push(axis, peer, src, dst, ssem, rsem):
        copy = pltpu.make_async_remote_copy(
            src_ref=src, dst_ref=dst, send_sem=ssem, recv_sem=rsem,
            device_id={axis: peer}, device_id_type=MESH,
        )
        copy.start()
        pending.append(copy)
        return copy

    def share(axis, me, n, buf, ssem, rsem, width=1):
        at = buf.at[pl.ds(me * width, width)]
        return [
            push(axis, flip(me, m), at, at, ssem.at[m - 1], rsem.at[m - 1])
            for m in range(n - 1, 0, -1)
        ]

    def arrive(copies):
        for copy in copies:
            copy.wait_recv()

    def total(buf, n):
        out = buf[0]
        for i in range(1, n):
            out = out + buf[i]
        return out

    def fold(gram):
        return jnp.concatenate([gram[:half], gram[half:]], axis=1)

    def unfold(packed):
        return jnp.concatenate([packed[:, :frames], packed[:, frames:]], axis=0)

    def put_panel(it, h, value):
        for b in range(cb):
            piece = value[span(h), b * BLOCK : (b + 1) * BLOCK]
            panels[h][it, r * cb + b] = piece.astype(bf16)

    def gather_rows(it, h):
        return share("row", r, nr, panels[h].at[it], ag_s.at[it, h], ag_r.at[it, h], cb)

    def sweep(source, it, h, weight, count, pick, flags):
        run = jnp.zeros((part, BLOCK), f32)
        for t in range(count):
            both = [source[it, tab[pick + g, t]] for g in range(2)]
            run = run * keep[flags, t] + lax.dot_general(
                jnp.concatenate(both, axis=1), weight(t), (((1,), (0,)), ((), ())),
                preferred_element_type=f32,
            )
            scan[h, t] = run

    def forward(it, h):
        sweep(panels[h], it, h, lambda t: turned[t], (kb + nrow) // 2, 2, 0)

    def backward(it, h):
        weight = lambda t: jnp.concatenate([blocks[tab[5 + g, t]] for g in range(2)], axis=0)
        sweep(feet[h], it, h, weight, (kb + ncol) // 2, 7, 2)

    def half_square(it, which):
        wide = jnp.concatenate(
            [
                jnp.concatenate(
                    [feet[p][it, which * hrow + j] for p in range(PARTS)], axis=0
                )
                for j in range(hrow)
            ],
            axis=1,
        )
        return lax.dot_general(
            wide, wide, (((1,), (1,)), ((), ())), preferred_element_type=f32
        )

    def segment(h, end_at, valid_at, i):
        return scan[h, tab[end_at, i]] * keep[valid_at, i]

    loads[0].wait()
    for h in range(PARTS):
        put_panel(0, h, rhs_ref[...])
    pl.semaphore_wait(barrier, nr + nc - 2)
    gather = [gather_rows(0, h) for h in range(PARTS)]
    loads[1].wait()
    loads[2].wait()
    eye = lax.broadcasted_iota(i32, (kb, kb), 0) == lax.broadcasted_iota(i32, (kb, kb), 1)
    stand = lambda row: jnp.sum(jnp.where(eye, row, 0), axis=1, keepdims=True)
    bi, bj = rowi[...], coli[...]
    row_key = lax.rem(bi, nrow)
    col_key = lax.div(bj, nrow) * cb + lax.rem(bj, cb)
    row_up, col_up = stand(row_key), stand(col_key)
    ints_r, flags_r = order_by(row_key, row_up, col_up, kb)
    ints_c, flags_c = order_by(col_key, col_up, row_up, kb)
    blank = [jnp.zeros((1, BLOCK), i32)]
    tabv[...] = jnp.concatenate(ints_r + ints_c + blank * 6, axis=0)
    keepv[...] = jnp.concatenate(flags_r + flags_c + blank * 4, axis=0).astype(f32)
    tables = [
        pltpu.make_async_copy(tabv, tab, tab_sem.at[0]),
        pltpu.make_async_copy(keepv, keep, tab_sem.at[1]),
    ]
    for copy in tables:
        copy.start()
    loads[3].wait()
    rhs = rhs_ref[...]
    gca[c, :, :frames] = pair_gram(rhs, rhs)
    gca[c, :, frames:] = pair_gram(rhs, prior_ref[...] * rhs)
    gram_cols = share("col", c, nc, gca, ga_s, ga_r)
    for copy in tables:
        copy.wait()
    loads[4].wait()

    def turn(t, _):
        for g in range(2):
            turned[t, g * BLOCK : (g + 1) * BLOCK] = blocks[tab[g, t]].T
        return 0

    lax.fori_loop(0, (kb + nrow) // 2, turn, 0, unroll=8)
    arrive(gram_cols)
    sums = total(gca, nc)
    gra[r] = fold(sums[:, :frames])
    weighted = fold(sums[:, frames:])
    gram = inverse = alpha = None

    for it in range(ITERS):
        last = it + 1 == ITERS
        if it > 0:
            arrive(gram_cols)
            grb[it - 1, r] = total(gcb.at[it - 1], nc)
            gram_rows = share(
                "row", r, nr, grb.at[it - 1], grb_s.at[it - 1], grb_r.at[it - 1]
            )
        crossed = []
        for h in range(PARTS):
            arrive(gather[h])
            if it == 0 and h + 1 == PARTS:
                gram_rows = share("row", r, nr, gra, gb_s, gb_r)
            forward(it, h)
            for j in range(hrow):
                csend[it, h, j] = segment(h, 4, 1, (1 - side) * hrow + j).astype(bf16)
            swapped = push(
                "col", flip(c, 1), csend.at[it, h], cland.at[it, h],
                ch_s.at[it, h], ch_r.at[it, h],
            )
            arrive([swapped])
            for j in range(hrow):
                own = segment(h, 4, 1, side * hrow + j) + cland[it, h, j].astype(f32)
                pair[h, j] = own
                xsend[it, h, j] = own.astype(bf16)
            crossed.append([
                push(
                    "col", flip(c, 2 * m + m % 2), xsend.at[it, h], xland.at[it, h, m - 1],
                    xh_s.at[it, h, m - 1], xh_r.at[it, h, m - 1],
                )
                for m in range(nx - 1, 0, -1)
            ])
        if it > 0:
            arrive(gram_rows)
            gram = unfold(total(grb.at[it - 1], nr))
            beta = dot(inverse, gram, ((1,), (0,)))
            adjust[...] = left_t(beta, foot[...])
        copies = []
        for h in range(PARTS):
            arrive(crossed[h])
            for j in range(hrow):
                at = slice(j * BLOCK, (j + 1) * BLOCK)
                own = pair[h, j]
                for m in range(nx - 1):
                    own = own + xland[it, h, m, j].astype(f32)
                if it > 0:
                    own = own + adjust[span(h), at]
                if not last:
                    foot[span(h), at] = own
                feet[h][it, side * hrow + j] = own.astype(bf16)
            at = feet[h].at[it, pl.ds(side * hrow, hrow)]
            spread = push("col", flip(c, 1), at, at, fg_s.at[it, h], fg_r.at[it, h])
            if it > 0 and h == 0:
                before = (rhs_ref if it == 1 else direct)[...]
                direct[...] = resid[...] + left_t(beta, before)
                direction = direct[...]
                gcc[it - 1, c] = fold(pair_gram(direction, prior_ref[...] * direction))
                weight_cols = share(
                    "col", c, nc, gcc.at[it - 1], gcc_s.at[it - 1], gcc_r.at[it - 1]
                )
            if h + 1 == PARTS:
                square = half_square(it, side)
            arrive([spread])
            if h + 1 == PARTS:
                square = square + half_square(it, 1 - side)
                if it > 0:
                    arrive(weight_cols)
                    weighted = total(gcc.at[it - 1], nc)
                grk[it, r] = fold(square) + weighted
                curve_rows = share("row", r, nr, grk.at[it], gk_s.at[it], gk_r.at[it])
            backward(it, h)
            for i in range(ncol):
                sendb[it, h, i] = segment(h, 9, 3, i).astype(bf16)
            copies.append([
                push(
                    "row", flip(r, m), sendb.at[it, h, pl.ds(flip(r, m) * cb, cb)],
                    landb.at[it, h, m - 1], br_s.at[it, h, m - 1], br_r.at[it, h, m - 1],
                )
                for m in range(nr - 1, 0, -1)
            ])
        if it == 0:
            arrive(gram_rows)
            gram = unfold(total(gra, nr))
        if not last:
            square = (frames, frames)
            ones = lax.broadcasted_iota(i32, square, 0) == lax.broadcasted_iota(i32, square, 1)
            inverse = gauss_jordan(jnp.where(ones, 1.0, 0.0), gram, frames)
        now = rhs_ref if it == 0 else direct
        for h in range(PARTS):
            if h + 1 == PARTS:
                arrive(curve_rows)
                alpha = gauss_jordan(gram, unfold(total(grk.at[it], nr)), frames)
                if last:
                    update = left_t(alpha, now[...])
                    sol_ref[...] = update if it == 0 else sol_ref[...] + update
            arrive(copies[h])
            for b in range(cb):
                at = slice(b * BLOCK, (b + 1) * BLOCK)
                own = segment(h, 9, 3, r * cb + b)
                for o in range(nr - 1):
                    own = own + landb[it, h, o, b].astype(f32)
                image[span(h), at] = own + prior_ref[:, at] * now[span(h), at]
        residual = (rhs_ref if it == 0 else resid)[...] - left_t(alpha, image[...])
        if last:
            res_ref[...] = residual
        else:
            gather = []
            for h in range(PARTS):
                put_panel(it + 1, h, residual)
                gather.append(gather_rows(it + 1, h))
            resid[...] = residual
            gcb[it, c] = fold(pair_gram(residual, residual))
            gram_cols = share("col", c, nc, gcb.at[it], gcb_s.at[it], gcb_r.at[it])
            update = left_t(alpha, now[...])
            sol_ref[...] = update if it == 0 else sol_ref[...] + update
    for copy in pending:
        copy.wait_send()


def store(sol, res, sol_hbm, res_hbm, sem):
    copies = [
        pltpu.make_async_copy(src, dst, sem.at[i])
        for i, (src, dst) in enumerate(((sol, sol_hbm), (res, res_hbm)))
    ]
    for copy in copies:
        copy.start()
    for copy in copies:
        copy.wait()


def in_hbm(array):
    return pltpu.with_memory_space_constraint(array, pltpu.HBM)


def shards(right_side, prior, blocks, block_row, block_col):
    frames, pix = right_side.shape
    kb = blocks.shape[0]
    cb = pix // BLOCK
    nr = lax.axis_size("row")
    nc = lax.axis_size("col")
    nrow, ncol = cb * nc, cb * nr
    hrow, nx = nrow // 2, nc // 2
    vm = pl.BlockSpec(memory_space=pltpu.VMEM)
    dma = pltpu.SemaphoreType.DMA
    tile = (frames // PARTS, BLOCK)
    pieces = (ITERS, PARTS)
    half = (frames // 2, 2 * frames)
    out = jax.ShapeDtypeStruct(right_side.shape, f32)
    made = pl.pallas_call(
        functools.partial(kernel, nr, nc, cb, kb, frames),
        out_shape=(out, out),
        in_specs=[pl.BlockSpec(memory_space=pltpu.HBM)] * 5,
        out_specs=(vm, vm),
        scratch_shapes=[
            pltpu.VMEM((1, kb), i32),
            pltpu.VMEM((1, kb), i32),
            pltpu.VMEM((16, BLOCK), i32),
            pltpu.VMEM((8, BLOCK), f32),
            pltpu.SMEM((16, BLOCK), i32),
            pltpu.SMEM((8, BLOCK), f32),
            pltpu.VMEM(right_side.shape, f32),
            pltpu.VMEM((1, pix), f32),
            pltpu.VMEM((kb + 1, BLOCK, BLOCK), bf16),
            pltpu.VMEM(((kb + nrow) // 2, 2 * BLOCK, BLOCK), bf16),
            [pltpu.VMEM((ITERS, ncol) + tile, bf16)] * PARTS,
            [pltpu.VMEM((ITERS, nrow) + tile, bf16)] * PARTS,
            pltpu.VMEM(pieces + (hrow,) + tile, bf16),
            pltpu.VMEM(pieces + (hrow,) + tile, bf16),
            pltpu.VMEM(pieces + (hrow,) + tile, bf16),
            pltpu.VMEM(pieces + (nx - 1, hrow) + tile, bf16),
            pltpu.VMEM((PARTS, hrow) + tile, f32),
            pltpu.VMEM(pieces + (ncol,) + tile, bf16),
            pltpu.VMEM(pieces + (nr - 1, cb) + tile, bf16),
            pltpu.VMEM((PARTS, (kb + max(nrow, ncol)) // 2) + tile, f32),
            pltpu.VMEM(right_side.shape, f32),
            pltpu.VMEM(right_side.shape, f32),
            pltpu.VMEM(right_side.shape, f32),
            pltpu.VMEM((frames, hrow * BLOCK), f32),
            pltpu.VMEM((frames, hrow * BLOCK), f32),
            pltpu.VMEM((nc, frames, 2 * frames), f32),
            pltpu.VMEM((nr,) + half, f32),
            pltpu.VMEM((ITERS - 1, nc) + half, f32),
            pltpu.VMEM((ITERS - 1, nr) + half, f32),
            pltpu.VMEM((ITERS - 1, nc) + half, f32),
            pltpu.VMEM((ITERS, nr) + half, f32),
            dma((5,)),
            dma((2,)),
            dma(pieces + (nr - 1,)), dma(pieces + (nr - 1,)),
            dma(pieces), dma(pieces),
            dma(pieces + (nx - 1,)), dma(pieces + (nx - 1,)),
            dma(pieces), dma(pieces),
            dma(pieces + (nr - 1,)), dma(pieces + (nr - 1,)),
            dma((nc - 1,)), dma((nc - 1,)),
            dma((nr - 1,)), dma((nr - 1,)),
            dma((ITERS - 1, nc - 1)), dma((ITERS - 1, nc - 1)),
            dma((ITERS - 1, nr - 1)), dma((ITERS - 1, nr - 1)),
            dma((ITERS - 1, nc - 1)), dma((ITERS - 1, nc - 1)),
            dma((ITERS, nr - 1)), dma((ITERS, nr - 1)),
        ],
        compiler_params=pltpu.CompilerParams(
            collective_id=0, has_side_effects=True, vmem_limit_bytes=32 << 20
        ),
    )(*map(in_hbm, (block_row[None, :], block_col[None, :], right_side, prior[None, :], blocks)))
    return pl.pallas_call(
        store,
        out_shape=(out, out),
        in_specs=[pl.BlockSpec(memory_space=pl.ANY)] * 2,
        out_specs=(pl.BlockSpec(memory_space=pltpu.HBM),) * 2,
        scratch_shapes=[dma((2,))],
        compiler_params=pltpu.CompilerParams(vmem_limit_bytes=1 << 20),
    )(*made)


def solution(mesh):
    return jax.shard_map(
        shards,
        mesh=mesh,
        in_specs=(
            P("groups", ("row", "col")),
            P(("row", "col")),
            P(("row", "col"), None, None),
            P(("row", "col")),
            P(("row", "col")),
        ),
        out_specs=(P("groups", ("row", "col")), P("groups", ("row", "col"))),
        check_vma=False,
    )
```
